128 devices in a mesh: gx: 8 (over y, core), gy: 16 (over z, x).
Axes of the slice: x: 4, y: 4, z: 4, core: 2. Of those that a mesh axis runs over, the one named last changes fastest.
Arguments:
- features: bfloat16 [1024, 110592], P('gx', 'gy'), may hold values from -6 to 6
- first_weight: bfloat16 [110592, 768], P(('gy', 'gx')), may hold values from -0.01953125 to 0.01953125
- second_weight: bfloat16 [768, 512], replicated, may hold values from -0.21875 to 0.21875
- centres: bfloat16 [622592, 512], P(('gx', 'gy')), may hold values from -6 to 6
- active: int32 [622592], P(('gx', 'gy')), may hold values from 0 to 16127, as said below
- labels: int32 [1024], replicated, may hold values from 0 to 2064383, as said below
Outputs:
- loss: float32 [], replicated
- grad_first: bfloat16 [110592, 768], P(('gy', 'gx'))
- grad_second: bfloat16 [768, 512], replicated
- grad_centres: bfloat16 [622592, 512], P(('gx', 'gy'))
The draws below stay inside these ranges and needn't reach their ends.
Inputs may be any that keep to these rules, and one draw needn't show every extreme that they name: Each shard's 4864 entries are distinct and increasing; entry c names class (c // 4864) * 16128 + active[c]. `labels`: every image's class is among the sampled classes, so exactly one centre matches it.
All inputs are finite; a program needn't handle non-finite values.
Results may differ from the reference program's by a relative error of at most 0.0075.
Values may be sent and summed in bfloat16 or wider, within the bound.
A program may use at most 128 MiB of HBM per device.

```python
import jax
import jax.numpy as jnp
from jax import lax

F = 110592
H = 768
E = 512
CLS_DEV = 16128
CEN_DEV = 4864
B = 1024
CENTRES = 622592
NCLASS = 2064384
N_GX = 8
N_GY = 16


def choose_classes(key):
    base = jax.random.fold_in(key, 7)
    label_key, order_key = jax.random.split(base)
    shard_count = NCLASS // CLS_DEV
    labels = jax.random.randint(label_key, (B,), 0, NCLASS).astype(jnp.int32)
    labels = labels.at[0].set(0).at[B - 1].set(NCLASS - 1)
    marked = jnp.zeros((NCLASS,), jnp.int32).at[labels].set(1).reshape(shard_count, CLS_DEV)
    local_ids = jnp.arange(CLS_DEV, dtype=jnp.int32)[None, :]
    ends = ((local_ids == 0) | (local_ids == CLS_DEV - 1)).astype(jnp.int32)
    boosted = jnp.maximum(marked, ends)
    scores = jax.random.randint(order_key, (shard_count, CLS_DEV), 0, 16384).astype(jnp.int32) * CLS_DEV + local_ids
    scores = scores + boosted * 2 ** 28
    chosen = lax.top_k(scores, CEN_DEV)[1].astype(jnp.int32)
    chosen = jnp.sort(chosen, axis=1)
    return (labels, chosen.reshape(-1))


def draw_active(key, part):
    return choose_classes(key)[1]


def draw_labels(key, part):
    return choose_classes(key)[0]


def block_levels(stream_key, extent, cuts, low, top_value):
    loudness, own = 1.0, jax.random.fold_in(stream_key, 6)
    for position, shards_of in cuts:
        steps = jnp.exp(jax.random.uniform(jax.random.fold_in(own, position), (shards_of,), jnp.float32, low / len(cuts), top_value / len(cuts)))
        loudness = loudness * jnp.repeat(steps, extent[position] // shards_of).reshape([-1 if axis == position else 1 for axis in range(len(extent))])
    return loudness


def bell_draw(key, dims, width, reach, cuts=(), kind=jnp.bfloat16):
    values = jax.random.normal(key, dims, jnp.float32) * width
    if len(cuts) > 0:
        values = block_levels(key, dims, cuts, -0.22, 0.18) * values
    return jnp.clip(values, min=-reach, max=reach).astype(kind)


def setup_inputs(seed: int = 0) -> dict:
    streams_of = jax.random.split(jax.random.key(seed), 7)
    return {
        "features": bell_draw(streams_of[0], (B, F), 1.0, 6.0, ((0, 8), (1, 16))),
        "first_weight": bell_draw(streams_of[1], (F, H), F ** -0.5, 0.01953125, ((0, 128),)),
        "second_weight": bell_draw(streams_of[2], (H, E), H ** -0.5, 0.21875),
        "centres": bell_draw(streams_of[3], (CENTRES, E), 1.0, 6.0, ((0, 128),)),
        "active": draw_active(jax.random.fold_in(streams_of[6], 71), 0),
        "labels": draw_labels(jax.random.fold_in(streams_of[6], 71), 0),
    }


LOGIT_SCALE = 64.0
COS_MARGIN = 0.4
NORM_EPSILON = 1e-06

def reference(features, first_weight, second_weight, centres, active, labels):
    hidden = jnp.dot(features, first_weight, preferred_element_type=jnp.float32)
    activation, gelu_back = jax.vjp(jax.nn.gelu, hidden)
    act_half = activation.astype(jnp.bfloat16)
    embedding = jnp.dot(act_half, second_weight, preferred_element_type=jnp.float32)
    inv_embed = lax.rsqrt(lax.optimization_barrier(jnp.sum(embedding * embedding, axis=1, keepdims=True)) + NORM_EPSILON)
    unit = embedding * inv_embed
    unit_half = unit.astype(jnp.bfloat16)
    image_count = labels.shape[0]
    shards = N_GX * N_GY
    cen_blocks = centres.reshape(shards, CEN_DEV, centres.shape[1])
    act_blocks = active.reshape(shards, CEN_DEV)
    shard_ids = jnp.arange(shards, dtype=jnp.int32)

    def block_terms(shard, cen_block, act_block):
        cen = cen_block.astype(jnp.float32)
        inv_cen = lax.rsqrt(lax.optimization_barrier(jnp.sum(cen * cen, axis=1, keepdims=True)) + NORM_EPSILON)
        normed = cen * inv_cen
        normed_half = normed.astype(jnp.bfloat16)
        cosine = jnp.dot(unit_half, normed_half.T, preferred_element_type=jnp.float32)
        classes = (shard * CLS_DEV + act_block).astype(jnp.int32)
        positive = (labels[:, None] == classes[None, :]).astype(jnp.float32)
        logits = LOGIT_SCALE * (cosine - COS_MARGIN * positive)
        exp_terms = jnp.exp(logits - LOGIT_SCALE)
        return (inv_cen, normed, normed_half, positive, logits, exp_terms)

    def first_pass(sums, inputs):
        shard, cen_block, act_block = inputs
        parts = block_terms(shard, cen_block, act_block)
        positive, logits, exp_terms = (parts[3], parts[4], parts[5])
        return ((sums[0] + lax.optimization_barrier(jnp.sum(exp_terms, axis=1)), sums[1] + lax.optimization_barrier(jnp.sum(positive * logits, axis=1))), None)
    zeros = jnp.zeros((image_count,), jnp.float32)
    (totals, target), unused = lax.scan(first_pass, (zeros, zeros), (shard_ids, cen_blocks, act_blocks))

    def second_pass(sums, inputs):
        shard, cen_block, act_block = inputs
        inv_cen, normed, normed_half, positive, logits, exp_terms = block_terms(shard, cen_block, act_block)
        weighted = jnp.dot(exp_terms.astype(jnp.bfloat16), normed_half, preferred_element_type=jnp.float32)
        picked = jnp.dot(positive.astype(jnp.bfloat16), normed_half, preferred_element_type=jnp.float32)
        coeff = (LOGIT_SCALE / image_count * (exp_terms / totals[:, None] - positive)).astype(jnp.bfloat16)
        grad_normed = jnp.dot(coeff.T, unit_half, preferred_element_type=jnp.float32)
        grad_cen = inv_cen * (grad_normed - normed * lax.optimization_barrier(jnp.sum(grad_normed * normed, axis=1, keepdims=True)))
        return ((sums[0] + weighted, sums[1] + picked), grad_cen.astype(jnp.bfloat16))
    zero_rows = jnp.zeros((image_count, unit.shape[1]), jnp.float32)
    (weighted, picked), grad_blocks = lax.scan(second_pass, (zero_rows, zero_rows), (shard_ids, cen_blocks, act_blocks))
    grad_centres = grad_blocks.reshape(centres.shape)
    grad_unit = LOGIT_SCALE / image_count * (weighted / totals[:, None] - picked)
    grad_embed = inv_embed * (grad_unit - unit * lax.optimization_barrier(jnp.sum(grad_unit * unit, axis=1, keepdims=True)))
    grad_embed_half = grad_embed.astype(jnp.bfloat16)
    grad_second = jnp.dot(act_half.T, grad_embed_half, preferred_element_type=jnp.float32).astype(jnp.bfloat16)
    grad_act = jnp.dot(grad_embed_half, second_weight.T, preferred_element_type=jnp.float32)
    grad_hidden, = gelu_back(grad_act)
    grad_hidden_half = grad_hidden.astype(jnp.bfloat16)
    grad_first = jnp.dot(features.T, grad_hidden_half, preferred_element_type=jnp.float32).astype(jnp.bfloat16)
    loss = jnp.mean(LOGIT_SCALE + jnp.log(totals) - target)
    return (loss, grad_first, grad_second, grad_centres)
```

```python
import functools

import jax
import jax.numpy as jnp
from jax import lax
from jax.experimental import pallas as pl
from jax.experimental.pallas import tpu as pltpu
from jax.sharding import PartitionSpec as P

CLS_DEV = 16128
LOGIT_SCALE = 64.0
COS_MARGIN = 0.4
NORM_EPSILON = 1e-06

MESH = pl.DeviceIdType.MESH
BF16 = jnp.bfloat16
F32 = jnp.float32
IMAGES = 1024
HIDDEN = 768
EMBED = 512
BLOCK = 864
ORDERS = (("x", "y", "z"), ("y", "z", "x"), ("z", "x", "y"))


class Place:
    def __init__(self):
        gx, gy = lax.axis_index("gx"), lax.axis_index("gy")
        self.gx, self.gy = gx, gy
        self.core = lax.rem(gx, 2)
        self.pos = {"y": lax.div(gx, 2), "z": lax.div(gy, 4), "x": lax.rem(gy, 4)}

    def peer(self, axis, d):
        q = lax.rem(self.pos[axis] + d, 4)
        if axis == "y":
            return (q * 2 + self.core, self.gy)
        if axis == "z":
            return (self.gx, q * 4 + self.pos["x"])
        return (self.gx, self.pos["z"] * 4 + q)

    def partner(self):
        return (self.gx + 1 - 2 * self.core, self.gy)

    def row(self, d):
        return (lax.rem(self.gx + d, 8), self.gy)

    def greet(self, whole_row):
        barrier = pltpu.get_barrier_semaphore()
        devices = [self.peer(axis, d) for axis in ("x", "z") for d in (1, 2, 3)]
        if whole_row:
            devices += [self.row(d) for d in range(1, 8)]
        else:
            devices += [self.partner()] + [self.peer("y", d) for d in (1, 2, 3)]
        for device in devices:
            pl.semaphore_signal(barrier, inc=1, device_id=device, device_id_type=MESH)
        pl.semaphore_wait(barrier, len(devices))


def remote(src, dst, send, recv, device):
    return pltpu.make_async_remote_copy(
        src_ref=src, dst_ref=dst, send_sem=send, recv_sem=recv, device_id=device, device_id_type=MESH
    )


def each(count, size, body):
    def step(i, carry):
        body(pl.ds(pl.multiple_of(i * size, size), size))
        return carry

    lax.fori_loop(0, count // size, step, 0)


def sum_scratch(groups):
    return [
        pltpu.VMEM((groups, 1024, 128), F32),
        pltpu.VMEM((groups, 1024, 128), BF16),
        pltpu.VMEM((groups, 1024, 128), BF16),
        pltpu.VMEM((groups, 1024, 128), BF16),
        pltpu.VMEM((groups, 3, 256, 128), BF16),
        pltpu.VMEM((groups, 256, 128), F32),
        pltpu.VMEM((groups, 256, 128), BF16),
        pltpu.VMEM((groups, 3, 64, 128), BF16),
        pltpu.VMEM((groups, 64, 128), F32),
        pltpu.VMEM((groups, 64, 128), BF16),
        pltpu.VMEM((groups, 3, 16, 128), BF16),
        pltpu.SemaphoreType.DMA((groups, 8, 3)),
        pltpu.SemaphoreType.DMA((groups, 8, 3)),
    ]


def sum_everywhere(place, groups, bufs, out):
    acc, s0, r0, s1, r1, acc2, s2, r2, acc3, s3, r3, send, recv = bufs
    core = place.core
    started = []

    def go(src, dst, g, stage, k, device):
        copy = remote(src, dst, send.at[g, stage, k], recv.at[g, stage, k], device)
        copy.start()
        started.append(copy)
        return copy

    def scatter(g, stage, axis, sent, got, size):
        p = place.pos[axis]
        copies = []
        for d in (1, 2, 3):
            q = lax.rem(p + d, 4)
            rows = pl.ds(pl.multiple_of(q * size, size), size)
            copies.append(go(sent.at[g, rows], got.at[g, d - 1], g, stage, d - 1, place.peer(axis, d)))
        return copies

    live = [go(s0.at[g], r0.at[g], g, 0, 0, place.partner()) for g in range(groups)]
    nxt = []
    for g in range(groups):
        live[g].wait_recv()

        def add(rows, g=g):
            total = acc[g, rows, :] + r0[g, rows, :].astype(F32)
            acc[g, rows, :] = total
            s1[g, rows, :] = total.astype(BF16)

        each(1024, 128, add)
        nxt.append(scatter(g, 1, ORDERS[g][0], s1, r1, 256))
    live, nxt = nxt, []
    for g in range(groups):
        for copy in live[g]:
            copy.wait_recv()
        base = place.pos[ORDERS[g][0]] * 256

        def add(rows, g=g, base=base):
            own = pl.ds(pl.multiple_of(base + rows.start, 64), 64)
            total = acc[g, own, :] + (
                r1[g, 0, rows, :].astype(F32) + r1[g, 1, rows, :].astype(F32) + r1[g, 2, rows, :].astype(F32)
            )
            acc2[g, rows, :] = total
            s2[g, rows, :] = total.astype(BF16)

        each(256, 64, add)
        nxt.append(scatter(g, 2, ORDERS[g][1], s2, r2, 64))
    live, nxt = nxt, []
    for g in range(groups):
        for copy in live[g]:
            copy.wait_recv()
        own = pl.ds(pl.multiple_of(place.pos[ORDERS[g][1]] * 64, 64), 64)
        total = acc2[g, own, :] + (r2[g, 0].astype(F32) + r2[g, 1].astype(F32) + r2[g, 2].astype(F32))
        acc3[g] = total
        s3[g] = total.astype(BF16)
        nxt.append(scatter(g, 3, ORDERS[g][2], s3, r3, 16))
    live, nxt = nxt, []

    def spread(g, stage, axis, base, size):
        tile = core * groups + g
        rows = pl.ds(pl.multiple_of(base, size), size)
        part = out.at[tile, rows]
        return [go(part, part, g, stage, d - 1, place.peer(axis, d)) for d in (1, 2, 3)]

    bases = []
    for g in range(groups):
        for copy in live[g]:
            copy.wait_recv()
        p1, p2, p3 = (place.pos[axis] for axis in ORDERS[g])
        bases.append((p1 * 256 + p2 * 64 + p3 * 16, p1 * 256 + p2 * 64, p1 * 256))
        own = pl.ds(pl.multiple_of(p3 * 16, 16), 16)
        total = acc3[g, own, :] + (r3[g, 0].astype(F32) + r3[g, 1].astype(F32) + r3[g, 2].astype(F32))
        out[core * groups + g, pl.ds(pl.multiple_of(bases[g][0], 16), 16), :] = total.astype(BF16)
        nxt.append(spread(g, 4, ORDERS[g][2], bases[g][0], 16))
    for stage, which, size in ((5, 1, 64), (6, 0, 256)):
        live, nxt = nxt, []
        for g in range(groups):
            for copy in live[g]:
                copy.wait_recv()
            nxt.append(spread(g, stage, ORDERS[g][which], bases[g][2 - which], size))
    live, last = nxt, []
    for g in range(groups):
        for copy in live[g]:
            copy.wait_recv()
        whole = out.at[core * groups + g]
        last.append(go(whole, whole, g, 7, 0, place.partner()))
    for copy in last:
        copy.wait_recv()
    for copy in started:
        copy.wait_send()


def project_kernel(features, weight, hidden, blocks, sends, send_sem, recv_sem, *bufs):
    place = Place()
    place.greet(True)
    me = place.gx
    for j in range(8):
        piece = features[:, j * BLOCK : (j + 1) * BLOCK]
        sends[j] = piece
    copies = {}
    for d in (4, 5, 3, 2, 6, 7, 1):
        j = lax.rem(me + d, 8)
        copies[d] = remote(
            sends.at[j],
            blocks.at[pl.ds(pl.multiple_of(me * 128, 128), 128)],
            send_sem.at[d],
            recv_sem.at[d],
            place.row(d),
        )
        copies[d].start()
    blocks[pl.ds(pl.multiple_of(me * 128, 128), 128), :] = sends[me]
    acc, s0 = bufs[0], bufs[1]
    mine = pl.ds(pl.multiple_of(place.core * 384, 128), 384)
    theirs = pl.ds(pl.multiple_of((1 - place.core) * 384, 128), 384)
    for d in range(1, 8):
        copies[d].wait_recv()

    def product(rows):
        block = blocks[rows, :]
        own = jnp.dot(block, weight[:, mine], preferred_element_type=F32)
        other = jnp.dot(block, weight[:, theirs], preferred_element_type=F32)
        for g in range(3):
            acc[g, rows, :] = own[:, g * 128 : (g + 1) * 128]
            s0[g, rows, :] = other[:, g * 128 : (g + 1) * 128].astype(BF16)

    each(1024, 256, product)
    sum_everywhere(place, 3, bufs, hidden)
    for d in range(1, 8):
        copies[d].wait_send()


def project(features, weight):
    return pl.pallas_call(
        project_kernel,
        out_shape=(
            jax.ShapeDtypeStruct((6, IMAGES, 128), BF16),
            jax.ShapeDtypeStruct((IMAGES, BLOCK), BF16),
        ),
        in_specs=[pl.BlockSpec(memory_space=pltpu.VMEM)] * 2,
        out_specs=[pl.BlockSpec(memory_space=pltpu.VMEM)] * 2,
        scratch_shapes=[
            pltpu.VMEM((8, 128, BLOCK), BF16),
            pltpu.SemaphoreType.DMA((8,)),
            pltpu.SemaphoreType.DMA((8,)),
        ]
        + sum_scratch(3),
        compiler_params=pltpu.CompilerParams(collective_id=0, has_side_effects=True),
    )(features, weight)


def embed_kernel(term, out, *bufs):
    place = Place()
    place.greet(False)
    acc, s0 = bufs[0], bufs[1]

    def split(rows):
        for g in range(2):
            mine = pl.ds(pl.multiple_of(place.core * 256 + g * 128, 128), 128)
            theirs = pl.ds(pl.multiple_of((1 - place.core) * 256 + g * 128, 128), 128)
            acc[g, rows, :] = term[rows, mine]
            s0[g, rows, :] = term[rows, theirs].astype(BF16)

    each(1024, 128, split)
    sum_everywhere(place, 2, bufs, out)


def embed_sum(term):
    return pl.pallas_call(
        embed_kernel,
        out_shape=jax.ShapeDtypeStruct((4, IMAGES, 128), BF16),
        in_specs=[pl.BlockSpec(memory_space=pltpu.VMEM)],
        out_specs=pl.BlockSpec(memory_space=pltpu.VMEM),
        scratch_shapes=sum_scratch(2),
        compiler_params=pltpu.CompilerParams(collective_id=1, has_side_effects=True),
    )(term)


def pair_sums(place, value, got, send, recv):
    started = []
    for stage, axis in enumerate(("core", "x", "y", "z")):
        p = place.core if axis == "core" else place.pos[axis]
        got[stage, p] = value
        copies = []
        for d in (1,) if axis == "core" else (1, 2, 3):
            device = place.partner() if axis == "core" else place.peer(axis, d)
            slot = got.at[stage, p]
            copies.append(remote(slot, slot, send.at[stage, d - 1], recv.at[stage, d - 1], device))
            copies[-1].start()
        for copy in copies:
            copy.wait_recv()
        started += copies
        value = got[stage, 0] + got[stage, 1]
        if axis != "core":
            value = value + (got[stage, 2] + got[stage, 3])
    for copy in started:
        copy.wait_send()
    return value


def totals_kernel(pair, out, got, send, recv):
    place = Place()
    place.greet(False)
    out[...] = pair_sums(place, pair[...], got, send, recv)


def totals_sum(pair):
    return pl.pallas_call(
        totals_kernel,
        out_shape=jax.ShapeDtypeStruct((2, IMAGES), F32),
        in_specs=[pl.BlockSpec(memory_space=pltpu.VMEM)],
        out_specs=pl.BlockSpec(memory_space=pltpu.VMEM),
        scratch_shapes=[
            pltpu.VMEM((4, 4, 2, IMAGES), F32),
            pltpu.SemaphoreType.DMA((4, 3)),
            pltpu.SemaphoreType.DMA((4, 3)),
        ],
        compiler_params=pltpu.CompilerParams(collective_id=2, has_side_effects=True),
    )(pair)


def shards(features, first_weight, second_weight, centres, active, labels):
    device = lax.axis_index("gx") * lax.axis_size("gy") + lax.axis_index("gy")
    image_count = labels.shape[0]
    hidden_tiles, block_rows = project(features, first_weight)
    hidden = jnp.transpose(hidden_tiles, (1, 0, 2)).reshape(IMAGES, HIDDEN).astype(F32)
    activation, gelu_back = jax.vjp(jax.nn.gelu, hidden)
    act_half = activation.astype(BF16)
    embedding = jnp.dot(act_half, second_weight, preferred_element_type=F32)
    inv_embed = lax.rsqrt(jnp.sum(embedding * embedding, axis=1, keepdims=True) + NORM_EPSILON)
    unit = embedding * inv_embed
    unit_half = unit.astype(BF16)
    cen = centres.astype(F32)
    inv_cen = lax.rsqrt(jnp.sum(cen * cen, axis=1, keepdims=True) + NORM_EPSILON)
    normed = cen * inv_cen
    normed_half = normed.astype(BF16)
    cosine = jnp.dot(unit_half, normed_half.T, preferred_element_type=F32)
    classes = device * CLS_DEV + active
    matches = labels[:, None] == classes[None, :]
    positive = matches.astype(F32)
    logits = LOGIT_SCALE * (cosine - COS_MARGIN * positive)
    exp_terms = jnp.exp(logits - LOGIT_SCALE)
    row_total = jnp.sum(exp_terms, axis=1)
    row_target = jnp.sum(positive * logits, axis=1)
    pair = totals_sum(jnp.stack([row_total, row_target]))
    totals, target = pair[0], pair[1]
    factor = LOGIT_SCALE / image_count
    coeff = (factor * (exp_terms / totals[:, None] - positive)).astype(BF16)
    term = jnp.dot(coeff, normed_half, preferred_element_type=F32)
    grad_tiles = embed_sum(term)
    grad_unit = jnp.transpose(grad_tiles, (1, 0, 2)).reshape(IMAGES, EMBED).astype(F32)
    grad_normed = jnp.dot(coeff.T, unit_half, preferred_element_type=F32)
    grad_cen = inv_cen * (grad_normed - normed * jnp.sum(grad_normed * normed, axis=1, keepdims=True))
    loss = jnp.mean(LOGIT_SCALE + jnp.log(totals) - target)
    grad_embed = inv_embed * (grad_unit - unit * jnp.sum(grad_unit * unit, axis=1, keepdims=True))
    grad_embed_half = grad_embed.astype(BF16)
    grad_second = jnp.dot(act_half.T, grad_embed_half, preferred_element_type=F32)
    grad_act = jnp.dot(grad_embed_half, second_weight.T, preferred_element_type=F32)
    (grad_hidden,) = gelu_back(grad_act)
    grad_first = jnp.dot(block_rows.T, grad_hidden.astype(BF16), preferred_element_type=F32)
    return (loss, grad_first.astype(BF16), grad_second.astype(BF16), grad_cen.astype(BF16))


def solution(mesh):
    placed = (
        P("gx", "gy"),
        P(("gy", "gx"), None),
        P(),
        P(("gx", "gy"), None),
        P(("gx", "gy")),
        P(),
    )
    return jax.shard_map(
        shards,
        mesh=mesh,
        in_specs=placed,
        out_specs=(P(), P(("gy", "gx"), None), P(), P(("gx", "gy"), None)),
        check_vma=False,
    )
```

```python
import jax
import jax.numpy as jnp
from jax import lax
from jax.experimental import pallas as pl
from jax.experimental.pallas import tpu as pltpu
from jax.sharding import PartitionSpec as P

CLS_DEV = 16128
LOGIT_SCALE = 64.0
COS_MARGIN = 0.4
NORM_EPSILON = 1e-06

MESH = pl.DeviceIdType.MESH
BF16 = jnp.bfloat16
F32 = jnp.float32
IMAGES = 1024
HIDDEN = 768
EMBED = 512
BLOCK = 864
CENTRES = 4864
FACTOR = LOGIT_SCALE / IMAGES
LOG2E = 1.4426950408889634
ROOT = 0.7978845608028654
CUBIC = 0.044715
ORDERS = (("x", "y", "z"), ("y", "z", "x"), ("z", "x", "y"))
TILE = 256


class Place:
    def __init__(self):
        gx, gy = lax.axis_index("gx"), lax.axis_index("gy")
        self.gx, self.gy = gx, gy
        self.core = lax.rem(gx, 2)
        self.pos = {"y": lax.div(gx, 2), "z": lax.div(gy, 4), "x": lax.rem(gy, 4)}

    def peer(self, axis, d):
        q = lax.rem(self.pos[axis] + d, 4)
        if axis == "y":
            return (q * 2 + self.core, self.gy)
        if axis == "z":
            return (self.gx, q * 4 + self.pos["x"])
        return (self.gx, self.pos["z"] * 4 + q)

    def partner(self):
        return (self.gx + 1 - 2 * self.core, self.gy)

    def row(self, d):
        return (lax.rem(self.gx + d, 8), self.gy)

    def greet(self):
        barrier = pltpu.get_barrier_semaphore()
        devices = [self.peer(axis, d) for axis in ("x", "z") for d in (1, 2, 3)]
        devices += [self.row(d) for d in range(1, 8)]
        for device in devices:
            pl.semaphore_signal(barrier, inc=1, device_id=device, device_id_type=MESH)
        pl.semaphore_wait(barrier, len(devices))


def remote(src, dst, send, recv, device):
    return pltpu.make_async_remote_copy(
        src_ref=src, dst_ref=dst, send_sem=send, recv_sem=recv, device_id=device, device_id_type=MESH
    )


def block(index, size):
    return pl.ds(pl.multiple_of(index * size, size), size)


def each(count, body, start=0):
    def step(i, carry):
        body(i)
        return carry

    lax.fori_loop(start, start + count, step, 0)


def sum_scratch(groups):
    return [
        pltpu.VMEM((groups, 1024, 128), F32),
        pltpu.VMEM((groups, 1024, 128), BF16),
        pltpu.VMEM((groups, 1024, 128), BF16),
        pltpu.VMEM((groups, 1024, 128), BF16),
        pltpu.VMEM((groups, 3, 256, 128), BF16),
        pltpu.VMEM((groups, 256, 128), F32),
        pltpu.VMEM((groups, 3, 64, 128), F32),
        pltpu.VMEM((groups, 64, 128), F32),
        pltpu.VMEM((groups, 3, 16, 128), F32),
        pltpu.SemaphoreType.DMA((groups, 8, 3)),
        pltpu.SemaphoreType.DMA((groups, 8, 3)),
    ]


def sum_everywhere(place, groups, bufs, out, fill):
    acc, s0, r0, s1, r1, acc2, r2, acc3, r3, send, recv = bufs
    core = place.core
    started = []

    def go(src, dst, g, stage, k, device):
        copy = remote(src, dst, send.at[g, stage, k], recv.at[g, stage, k], device)
        copy.start()
        started.append(copy)
        return copy

    def scatter(g, stage, axis, sent, got, size):
        copies = []
        for d in (1, 2, 3):
            rows = block(lax.rem(place.pos[axis] + d, 4), size)
            copies.append(go(sent.at[g, rows], got.at[g, d - 1], g, stage, d - 1, place.peer(axis, d)))
        return copies

    live = [go(s0.at[g], r0.at[g], g, 0, 0, place.partner()) for g in range(groups)]
    fill(0)
    nxt = []
    for g in range(groups):
        live[g].wait_recv()

        def add(i, g=g):
            rows = block(i, 128)
            total = acc[g, rows, :] + r0[g, rows, :].astype(F32)
            acc[g, rows, :] = total
            s1[g, rows, :] = total.astype(BF16)

        each(8, add)
        nxt.append(scatter(g, 1, ORDERS[g][0], s1, r1, 256))
    live, nxt = nxt, []
    fill(1)
    for g in range(groups):
        for copy in live[g]:
            copy.wait_recv()
        own = block(place.pos[ORDERS[g][0]], 256)
        acc2[g] = acc[g, own, :] + (r1[g, 0].astype(F32) + r1[g, 1].astype(F32) + r1[g, 2].astype(F32))
        nxt.append(scatter(g, 2, ORDERS[g][1], acc2, r2, 64))
    live, nxt = nxt, []
    fill(2)
    for g in range(groups):
        for copy in live[g]:
            copy.wait_recv()
        own = block(place.pos[ORDERS[g][1]], 64)
        acc3[g] = acc2[g, own, :] + (r2[g, 0] + r2[g, 1] + r2[g, 2])
        nxt.append(scatter(g, 3, ORDERS[g][2], acc3, r3, 16))
    live, nxt = nxt, []
    fill(3)

    def spread(g, stage, axis, base, size):
        part = out.at[core * groups + g, pl.ds(pl.multiple_of(base, size), size)]
        return [go(part, part, g, stage, d - 1, place.peer(axis, d)) for d in (1, 2, 3)]

    bases = []
    for g in range(groups):
        for copy in live[g]:
            copy.wait_recv()
        p1, p2, p3 = (place.pos[axis] for axis in ORDERS[g])
        bases.append((p1 * 256 + p2 * 64 + p3 * 16, p1 * 256 + p2 * 64, p1 * 256))
        total = acc3[g, block(p3, 16), :] + (r3[g, 0] + r3[g, 1] + r3[g, 2])
        out[core * groups + g, pl.ds(pl.multiple_of(bases[g][0], 16), 16), :] = total.astype(BF16)
        nxt.append(spread(g, 4, ORDERS[g][2], bases[g][0], 16))
    for stage, which, size in ((5, 1, 64), (6, 0, 256)):
        live, nxt = nxt, []
        fill(stage - 1)
        for g in range(groups):
            for copy in live[g]:
                copy.wait_recv()
            nxt.append(spread(g, stage, ORDERS[g][which], bases[g][2 - which], size))
    live, last = nxt, []
    fill(6)
    for g in range(groups):
        for copy in live[g]:
            copy.wait_recv()
        whole = out.at[core * groups + g]
        last.append(go(whole, whole, g, 7, 0, place.partner()))
    fill(7)
    for copy in last:
        copy.wait_recv()
    return started


def pair_sums(place, value, got, send, recv, fill):
    started = []
    for stage, axis in enumerate(("core", "x", "y", "z")):
        p = place.core if axis == "core" else place.pos[axis]
        got[stage, p] = value
        copies = []
        for d in (1,) if axis == "core" else (1, 2, 3):
            device = place.partner() if axis == "core" else place.peer(axis, d)
            slot = got.at[stage, p]
            copies.append(remote(slot, slot, send.at[stage, d - 1], recv.at[stage, d - 1], device))
            copies[-1].start()
        fill(stage)
        for copy in copies:
            copy.wait_recv()
        started += copies
        value = got[stage, 0] + got[stage, 1]
        if axis != "core":
            value = value + (got[stage, 2] + got[stage, 3])
    return value, started


def gelu_parts(v):
    t = jnp.tanh(ROOT * (v + CUBIC * (v * v * v)))
    return 0.5 * (1.0 + t), t


def step_kernel(
    features_hbm, weight_hbm, second_hbm, centres_hbm, active, labels,
    loss, grad_first, grad_second, grad_centres,
    features, weight, second, centres, sends, blocks, turned, nh, nht, expt,
    hid, act, act_t, slope, unit, uh, inv_embed, gut, gu, ge, gh,
    sums, got, local_sem, out_sem, a2a_send, a2a_recv, pair_send, pair_recv, *bufs,
):
    one, two = bufs[:11], bufs[11:]
    place = Place()
    me = place.gx
    device = me * 16 + place.gy
    loads = [
        pltpu.make_async_copy(src, dst, local_sem.at[i])
        for i, (src, dst) in enumerate(
            ((features_hbm, features), (weight_hbm, weight), (centres_hbm, centres), (second_hbm, second))
        )
    ]
    for load in loads:
        load.start()
    place.greet()
    loads[0].wait()
    for j in range(8):
        sends[j] = features[:, j * BLOCK : (j + 1) * BLOCK]
    copies = {}
    for d in (4, 5, 3, 2, 6, 7, 1):
        copies[d] = remote(
            sends.at[lax.rem(me + d, 8)], blocks.at[block(me, 128)], a2a_send.at[d], a2a_recv.at[d], place.row(d)
        )
        copies[d].start()
    blocks[block(me, 128), :] = sends[me]

    loads[2].wait()

    def normalise(i):
        rows = block(i, 128)
        cen = centres[rows, :].astype(F32)
        normed = cen * lax.rsqrt(jnp.sum(cen * cen, axis=1, keepdims=True) + NORM_EPSILON)
        nh[rows, :] = normed.astype(BF16)
        nht[:, rows] = jnp.transpose(normed).astype(BF16)

    each(CENTRES // 128, normalise)
    loads[1].wait()
    acc, s0 = one[0], one[1]
    mine = pl.ds(pl.multiple_of(place.core * 384, 128), 384)
    theirs = pl.ds(pl.multiple_of((1 - place.core) * 384, 128), 384)
    for d in range(1, 8):
        copies[d].wait_recv()

    def product(i):
        rows = block(i, 256)
        piece = blocks[rows, :]
        own = jnp.dot(piece, weight[:, mine], preferred_element_type=F32)
        other = jnp.dot(piece, weight[:, theirs], preferred_element_type=F32)
        for g in range(3):
            acc[g, rows, :] = own[:, g * 128 : (g + 1) * 128]
            s0[g, rows, :] = other[:, g * 128 : (g + 1) * 128].astype(BF16)

    each(4, product)

    def turn(i):
        rows = block(i, 128)
        for k in range(0, BLOCK, 128):
            top = min(k + 128, BLOCK)
            turned[k:top, rows] = jnp.transpose(blocks[rows, k:top].astype(F32)).astype(BF16)

    def fill_one(stage):
        if stage == 1:
            each(8, turn)

    started = sum_everywhere(place, 3, one, hid, fill_one)
    loads[3].wait()

    def embed(i):
        rows = block(i, 256)
        for k in range(6):
            v = hid[k, rows, :].astype(F32)
            act[rows, k * 128 : (k + 1) * 128] = (v * gelu_parts(v)[0]).astype(BF16)
        emb = jnp.dot(act[rows, :], second[...], preferred_element_type=F32)
        inv = lax.rsqrt(jnp.sum(emb * emb, axis=1, keepdims=True) + NORM_EPSILON)
        inv_embed[rows, :] = inv
        u = emb * inv
        unit[rows, :] = u
        uh[rows, :] = u.astype(BF16)

    each(4, embed)
    sums[...] = jnp.zeros_like(sums)

    def positives(i, imgs):
        parts = []
        for k in range(TILE // 128):
            row = active[i * (TILE // 128) + k] + device * CLS_DEV
            column = jnp.transpose(jnp.broadcast_to(row, (128, 128)))
            parts.append(
                jnp.concatenate(
                    [column == labels[:, imgs + n * 128 : imgs + (n + 1) * 128] for n in range(2)], axis=1
                )
            )
        return jnp.concatenate(parts, axis=0)

    def forward(i):
        rows = block(i, TILE)
        for imgs in range(0, IMAGES, 256):
            cols = slice(imgs, imgs + 256)
            cosine = lax.dot_general(
                nh[rows, :], uh[cols, :], (((1,), (1,)), ((), ())), preferred_element_type=F32
            )
            match = positives(i, imgs)
            scale = LOGIT_SCALE * LOG2E
            shift = jnp.where(match, scale * (1.0 + COS_MARGIN), scale)
            exp_terms = jnp.exp2(scale * cosine - shift)
            hit = jnp.where(match, cosine - COS_MARGIN, 0.0)
            sums[0, :, cols] += jnp.sum(exp_terms.reshape(TILE // 8, 8, 256), axis=0)
            sums[1, :, cols] += jnp.sum(hit.reshape(TILE // 8, 8, 256), axis=0)
            expt[rows, cols] = exp_terms.astype(BF16)

    each(CENTRES // TILE, forward)

    def slopes(i):
        rows = block(i, 128)
        for k in range(6):
            v = hid[k, rows, :].astype(F32)
            half, t = gelu_parts(v)
            inner = ROOT * (1.0 + 3.0 * CUBIC * (v * v))
            slope[rows, k * 128 : (k + 1) * 128] = half + 0.5 * v * ((1.0 - t * t) * inner)
            act_t[k * 128 : (k + 1) * 128, rows] = jnp.transpose(v * half).astype(BF16)

    def fill_pair(stage):
        each(2, slopes, 2 * stage)

    pair = jnp.concatenate(
        [
            jnp.sum(sums[0], axis=0, keepdims=True),
            jnp.sum(sums[1], axis=0, keepdims=True) * LOGIT_SCALE,
        ],
        axis=0,
    )
    pair, more = pair_sums(place, pair, got, pair_send, pair_recv, fill_pair)
    started += more
    totals, target = pair[0:1, :], pair[1:2, :]
    loss[...] = jnp.sum(LOGIT_SCALE + jnp.log(totals) - target, axis=1, keepdims=True) * (1.0 / IMAGES)
    sums[0, 0:1, :] = FACTOR / totals
    gut[...] = jnp.zeros_like(gut)

    def backward(i):
        rows = block(i, TILE)
        for imgs in range(0, IMAGES, 256):
            cols = slice(imgs, imgs + 256)
            match = positives(i, imgs)
            coeff = expt[rows, cols].astype(F32) * sums[0, 0:1, cols] - jnp.where(match, FACTOR, 0.0)
            coeff = coeff.astype(BF16)
            expt[rows, cols] = coeff
            gut[:, cols] += jnp.dot(nht[:, rows], coeff, preferred_element_type=F32)

    each(CENTRES // TILE, backward)
    acc, s0 = two[0], two[1]

    def split(i):
        rows = block(i, 128)
        for g in range(2):
            mine = block(place.core * 2 + g, 128)
            theirs = block((1 - place.core) * 2 + g, 128)
            acc[g, rows, :] = jnp.transpose(gut[mine, rows])
            s0[g, rows, :] = jnp.transpose(gut[theirs, rows]).astype(BF16)

    each(8, split)

    def centre_grad(i):
        rows = block(i, TILE)
        grad_normed = jnp.dot(expt[rows, :], uh[...], preferred_element_type=F32)
        cen = centres[rows, :].astype(F32)
        inv = lax.rsqrt(jnp.sum(cen * cen, axis=1, keepdims=True) + NORM_EPSILON)
        normed = cen * inv
        along = jnp.sum(grad_normed * normed, axis=1, keepdims=True)
        nh[rows, :] = (inv * (grad_normed - normed * along)).astype(BF16)
        pltpu.make_async_copy(nh.at[rows], grad_centres.at[rows], out_sem.at[i]).start()

    share = (3, 5, 3, 2, 2, 2, 2, 0)

    def fill_two(stage):
        if share[stage]:
            each(share[stage], centre_grad, sum(share[:stage]))

    started += sum_everywhere(place, 2, two, gu, fill_two)

    def finish(i):
        rows = block(i, 256)
        g = jnp.concatenate([gu[k, rows, :] for k in range(4)], axis=1).astype(F32)
        u = unit[rows, :]
        along = jnp.sum(g * u, axis=1, keepdims=True)
        grad_embed = (inv_embed[rows, :] * (g - u * along)).astype(BF16)
        ge[rows, :] = grad_embed
        grad_act = lax.dot_general(
            grad_embed, second[...], (((1,), (1,)), ((), ())), preferred_element_type=F32
        )
        gh[rows, :] = (grad_act * slope[rows, :]).astype(BF16)

    each(4, finish)

    def first(i):
        rows = block(i, 288)
        grad_first[rows, :] = jnp.dot(turned[rows, :], gh[...], preferred_element_type=F32).astype(BF16)

    each(3, first)

    def second_grad(i):
        rows = block(i, 256)
        grad_second[rows, :] = jnp.dot(act_t[rows, :], ge[...], preferred_element_type=F32).astype(BF16)

    each(3, second_grad)

    def drain(i):
        rows = block(i, TILE)
        pltpu.make_async_copy(nh.at[rows], grad_centres.at[rows], out_sem.at[i]).wait()

    each(CENTRES // TILE, drain)
    for d in range(1, 8):
        copies[d].wait_send()
    for copy in started:
        copy.wait_send()


def shards(features, first_weight, second_weight, centres, active, labels):
    in_place = pl.BlockSpec(memory_space=pl.ANY)
    near = pl.BlockSpec(memory_space=pltpu.VMEM)
    dma = pltpu.SemaphoreType.DMA
    loss, grad_first, grad_second, grad_centres = pl.pallas_call(
        step_kernel,
        out_shape=(
            jax.ShapeDtypeStruct((1, 1), F32),
            jax.ShapeDtypeStruct((BLOCK, HIDDEN), BF16),
            jax.ShapeDtypeStruct((HIDDEN, EMBED), BF16),
            jax.ShapeDtypeStruct((CENTRES, EMBED), BF16),
        ),
        in_specs=[in_place] * 4 + [near] * 2,
        out_specs=(near, near, near, in_place),
        scratch_shapes=[
            pltpu.VMEM((128, 8 * BLOCK), BF16),
            pltpu.VMEM((BLOCK, HIDDEN), BF16),
            pltpu.VMEM((HIDDEN, EMBED), BF16),
            pltpu.VMEM((CENTRES, EMBED), BF16),
            pltpu.VMEM((8, 128, BLOCK), BF16),
            pltpu.VMEM((IMAGES, BLOCK), BF16),
            pltpu.VMEM((BLOCK, IMAGES), BF16),
            pltpu.VMEM((CENTRES, EMBED), BF16),
            pltpu.VMEM((EMBED, CENTRES), BF16),
            pltpu.VMEM((CENTRES, IMAGES), BF16),
            pltpu.VMEM((6, IMAGES, 128), BF16),
            pltpu.VMEM((IMAGES, HIDDEN), BF16),
            pltpu.VMEM((HIDDEN, IMAGES), BF16),
            pltpu.VMEM((IMAGES, HIDDEN), F32),
            pltpu.VMEM((IMAGES, EMBED), F32),
            pltpu.VMEM((IMAGES, EMBED), BF16),
            pltpu.VMEM((IMAGES, 1), F32),
            pltpu.VMEM((EMBED, IMAGES), F32),
            pltpu.VMEM((4, IMAGES, 128), BF16),
            pltpu.VMEM((IMAGES, EMBED), BF16),
            pltpu.VMEM((IMAGES, HIDDEN), BF16),
            pltpu.VMEM((2, 8, IMAGES), F32),
            pltpu.VMEM((4, 4, 2, IMAGES), F32),
            dma((4,)),
            dma((CENTRES // TILE,)),
            dma((8,)),
            dma((8,)),
            dma((4, 3)),
            dma((4, 3)),
        ]
        + sum_scratch(3)
        + sum_scratch(2),
        compiler_params=pltpu.CompilerParams(
            collective_id=0, has_side_effects=True, vmem_limit_bytes=67043328
        ),
    )(
        features,
        first_weight,
        second_weight,
        centres,
        active.reshape(CENTRES // 128, 1, 128),
        labels.reshape(1, IMAGES),
    )
    return loss.reshape(()), grad_first, grad_second, grad_centres


def solution(mesh):
    placed = (
        P("gx", "gy"),
        P(("gy", "gx"), None),
        P(),
        P(("gx", "gy"), None),
        P(("gx", "gy")),
        P(),
    )
    return jax.shard_map(
        shards,
        mesh=mesh,
        in_specs=placed,
        out_specs=(P(), P(("gy", "gx"), None), P(), P(("gx", "gy"), None)),
        check_vma=False,
    )
```

```python
import jax
import jax.numpy as jnp
from jax import lax
from jax.experimental import pallas as pl
from jax.experimental.pallas import tpu as pltpu
from jax.sharding import PartitionSpec as P

CLS_DEV = 16128
LOGIT_SCALE = 64.0
COS_MARGIN = 0.4
NORM_EPSILON = 1e-06

MESH = pl.DeviceIdType.MESH
BF16 = jnp.bfloat16
F32 = jnp.float32
IMAGES = 1024
HIDDEN = 768
EMBED = 512
BLOCK = 864
CENTRES = 4864
FACTOR = LOGIT_SCALE / IMAGES
LOG2E = 1.4426950408889634
ROOT = 0.7978845608028654
CUBIC = 0.044715
ORDERS = (("x", "y", "z"), ("y", "z", "x"), ("z", "x", "y"))
TILE = 256


class Place:
    def __init__(self):
        gx, gy = lax.axis_index("gx"), lax.axis_index("gy")
        self.gx, self.gy = gx, gy
        self.core = lax.rem(gx, 2)
        self.pos = {"y": lax.div(gx, 2), "z": lax.div(gy, 4), "x": lax.rem(gy, 4)}

    def peer(self, axis, d):
        q = lax.rem(self.pos[axis] + d, 4)
        if axis == "y":
            return (q * 2 + self.core, self.gy)
        if axis == "z":
            return (self.gx, q * 4 + self.pos["x"])
        return (self.gx, self.pos["z"] * 4 + q)

    def partner(self):
        return (self.gx + 1 - 2 * self.core, self.gy)

    def row(self, d):
        return (lax.rem(self.gx + d, 8), self.gy)

    def greet(self, meanwhile):
        barrier = pltpu.get_barrier_semaphore()
        devices = [self.peer(axis, d) for axis in ("x", "z") for d in (1, 2, 3)]
        devices += [self.row(d) for d in range(1, 8)]
        for device in devices:
            pl.semaphore_signal(barrier, inc=1, device_id=device, device_id_type=MESH)
        meanwhile()
        pl.semaphore_wait(barrier, len(devices))


def remote(src, dst, send, recv, device):
    return pltpu.make_async_remote_copy(
        src_ref=src, dst_ref=dst, send_sem=send, recv_sem=recv, device_id=device, device_id_type=MESH
    )


def block(index, size):
    return pl.ds(pl.multiple_of(index * size, size), size)


def each(count, body, start=0):
    def step(i, carry):
        body(i)
        return carry

    lax.fori_loop(start, start + count, step, 0)


def sum_scratch(groups):
    return [
        pltpu.VMEM((groups, 512, 128), F32),
        pltpu.VMEM((groups, 512, 128), F32),
        pltpu.VMEM((groups, 512, 128), F32),
        pltpu.VMEM((groups, 512, 128), BF16),
        pltpu.VMEM((groups, 3, 128, 128), BF16),
        pltpu.VMEM((groups, 128, 128), F32),
        pltpu.VMEM((groups, 3, 32, 128), F32),
        pltpu.VMEM((groups, 4, 32, 128), F32),
        pltpu.SemaphoreType.DMA((groups, 7, 3)),
        pltpu.SemaphoreType.DMA((groups, 7, 3)),
    ]


def sum_everywhere(place, half, groups, bufs, out, started):
    acc, s0, r0, s1, r1, acc2, r2, x3, send, recv = bufs
    core = place.core

    def go(src, dst, g, stage, k, device):
        copy = remote(src, dst, send.at[g, stage, k], recv.at[g, stage, k], device)
        copy.start()
        started.append(copy)
        return copy

    def scatter(g, stage, axis, sent, got, size):
        copies = []
        for d in (2, 1, 3):
            rows = block(lax.rem(place.pos[axis] + d, 4), size)
            copies.append(go(sent.at[g, rows], got.at[g, d - 1], g, stage, d - 1, place.peer(axis, d)))
        return copies

    def spread(g, stage, axis, base, size):
        part = out.at[core * groups + g, pl.ds(pl.multiple_of(base, size), size)]
        return [go(part, part, g, stage, d - 1, place.peer(axis, d)) for d in (2, 1, 3)]

    live = [go(s0.at[g], r0.at[g], g, 0, 0, place.partner()) for g in range(groups)]
    yield
    nxt = []
    for g in range(groups):
        live[g].wait_recv()

        def add(i, g=g):
            rows = block(i, 128)
            total = acc[g, rows, :] + r0[g, rows, :]
            acc[g, rows, :] = total
            s1[g, rows, :] = total.astype(BF16)

        each(4, add)
        nxt.append(scatter(g, 1, ORDERS[g][0], s1, r1, 128))
    live, nxt = nxt, []
    yield
    for g in range(groups):
        for copy in live[g]:
            copy.wait_recv()
        own = block(place.pos[ORDERS[g][0]], 128)
        acc2[g] = acc[g, own, :] + (r1[g, 0].astype(F32) + r1[g, 1].astype(F32) + r1[g, 2].astype(F32))
        nxt.append(scatter(g, 2, ORDERS[g][1], acc2, r2, 32))
    live, nxt = nxt, []
    yield
    for g in range(groups):
        for copy in live[g]:
            copy.wait_recv()
        own = block(place.pos[ORDERS[g][1]], 32)
        p = place.pos[ORDERS[g][2]]
        x3[g, p] = acc2[g, own, :] + (r2[g, 0] + r2[g, 1] + r2[g, 2])
        slot = x3.at[g, p]
        nxt.append([go(slot, slot, g, 3, d - 1, place.peer(ORDERS[g][2], d)) for d in (2, 1, 3)])
    live, nxt = nxt, []
    yield
    bases = []
    for g in range(groups):
        for copy in live[g]:
            copy.wait_recv()
        first = half * 512 + place.pos[ORDERS[g][0]] * 128
        bases.append((first + place.pos[ORDERS[g][1]] * 32, first))
        total = (x3[g, 0] + x3[g, 1]) + (x3[g, 2] + x3[g, 3])
        out[core * groups + g, pl.ds(pl.multiple_of(bases[g][0], 32), 32), :] = total.astype(BF16)
        nxt.append(spread(g, 4, ORDERS[g][1], bases[g][0], 32))
    live, nxt = nxt, []
    yield
    for g in range(groups):
        for copy in live[g]:
            copy.wait_recv()
        nxt.append(spread(g, 5, ORDERS[g][0], bases[g][1], 128))
    live, last = nxt, []
    yield
    for g in range(groups):
        for copy in live[g]:
            copy.wait_recv()
        whole = out.at[core * groups + g, pl.ds(half * 512, 512)]
        last.append(go(whole, whole, g, 6, 0, place.partner()))
    yield
    for copy in last:
        copy.wait_recv()


def pair_sums(place, value, got, send, recv, started, keep):
    for stage, axis in enumerate(("core", "x", "y", "z")):
        p = place.core if axis == "core" else place.pos[axis]
        got[stage, p] = value
        copies = []
        for d in (1,) if axis == "core" else (2, 1, 3):
            device = place.partner() if axis == "core" else place.peer(axis, d)
            slot = got.at[stage, p]
            copies.append(remote(slot, slot, send.at[stage, d - 1], recv.at[stage, d - 1], device))
            copies[-1].start()
        yield
        for copy in copies:
            copy.wait_recv()
        started += copies
        value = got[stage, 0] + got[stage, 1]
        if axis != "core":
            value = value + (got[stage, 2] + got[stage, 3])
    keep.append(value)


def gelu_parts(v):
    t = jnp.tanh(ROOT * (v + CUBIC * (v * v * v)))
    return 0.5 * (1.0 + t), t


def step_kernel(
    features_hbm, weight_hbm, second_hbm, centres_hbm, active, labels,
    loss, turned_hbm, gh_hbm, act_t_hbm, ge_hbm, grad_centres,
    features, weight, second, centres, sends, blocks, turned, nh, nht, expt,
    hid, act, act_t, slope, unit, uh, inv_embed, gut, gu, ge,
    sums, got, places, local_sem, out_sem, a2a_send, a2a_recv, pair_send, pair_recv, *bufs,
):
    size = len(bufs) // 4
    one, two = (bufs[:size], bufs[size : 2 * size]), (bufs[2 * size : 3 * size], bufs[3 * size :])
    place = Place()
    me = place.gx
    device = me * 16 + place.gy
    started, leaving = [], []
    loads = [
        pltpu.make_async_copy(src, dst, local_sem.at[i])
        for i, (src, dst) in enumerate(
            ((features_hbm, features), (centres_hbm, centres), (weight_hbm, weight), (second_hbm, second))
        )
    ]

    def leave(src, dst):
        leaving.append(pltpu.make_async_copy(src, dst, local_sem.at[4 + len(leaving)]))
        leaving[-1].start()

    def prepare():
        for load in loads:
            load.start()
        loads[0].wait()
        for j in range(8):
            sends[j] = features[:, j * BLOCK : (j + 1) * BLOCK]

    place.greet(prepare)
    copies = ({}, {})
    for half in range(2):
        for d in (4, 5, 3, 2, 6, 7, 1):
            copies[half][d] = remote(
                sends.at[lax.rem(me + d, 8), pl.ds(half * 64, 64)],
                blocks.at[pl.ds(pl.multiple_of(half * 512 + me * 64, 64), 64)],
                a2a_send.at[half, d],
                a2a_recv.at[half, d],
                place.row(d),
            )
            copies[half][d].start()
    for half in range(2):
        blocks[pl.ds(pl.multiple_of(half * 512 + me * 64, 64), 64), :] = sends[me, half * 64 : half * 64 + 64, :]
        for j in range(8):
            spot = half * 512 + j * 64
            places[:, spot : spot + 64] = labels[:, j * 128 + half * 64 : j * 128 + half * 64 + 64]
    sums[...] = jnp.zeros_like(sums)
    loads[1].wait()

    def normalise(i):
        rows = block(i, 128)
        cen = centres[rows, :].astype(F32)
        normed = cen * lax.rsqrt(jnp.sum(cen * cen, axis=1, keepdims=True) + NORM_EPSILON)
        nh[rows, :] = normed.astype(BF16)
        nht[:, rows] = jnp.transpose(normed).astype(BF16)

    def product(half):
        acc, s0 = one[half][0], one[half][1]
        mine = pl.ds(pl.multiple_of(place.core * 384, 128), 384)
        theirs = pl.ds(pl.multiple_of((1 - place.core) * 384, 128), 384)
        for d in range(1, 8):
            copies[half][d].wait_recv()

        def step(i):
            rows = block(i, 256)
            piece = blocks[pl.ds(pl.multiple_of(half * 512 + i * 256, 256), 256), :]
            other = jnp.dot(piece, weight[:, theirs], preferred_element_type=F32)
            own = jnp.dot(piece, weight[:, mine], preferred_element_type=F32)
            for g in range(3):
                acc[g, rows, :] = own[:, g * 128 : (g + 1) * 128]
                s0[g, rows, :] = other[:, g * 128 : (g + 1) * 128]

        each(2, step)
        return sum_everywhere(place, half, 3, one[half], hid, started)

    def turn(i):
        rows = block(i, 128)
        for k in range(0, BLOCK, 128):
            top = min(k + 128, BLOCK)
            turned[k:top, rows] = jnp.transpose(blocks[rows, k:top].astype(F32)).astype(BF16)

    def embed(i):
        rows = block(i, 256)
        for k in range(6):
            v = hid[k, rows, :].astype(F32)
            act[rows, k * 128 : (k + 1) * 128] = (v * gelu_parts(v)[0]).astype(BF16)
        emb = jnp.dot(act[rows, :], second[...], preferred_element_type=F32)
        inv = lax.rsqrt(jnp.sum(emb * emb, axis=1, keepdims=True) + NORM_EPSILON)
        inv_embed[rows, :] = inv
        u = emb * inv
        unit[rows, :] = u
        uh[rows, :] = u.astype(BF16)

    def columns(i):
        parts = []
        for k in range(TILE // 128):
            row = active[:, block(i * (TILE // 128) + k, 128)] + device * CLS_DEV
            parts.append(jnp.transpose(jnp.broadcast_to(row, (128, 128))))
        return jnp.concatenate(parts, axis=0)

    def matches(column, imgs):
        return jnp.concatenate(
            [column == places[:, imgs + n * 128 : imgs + (n + 1) * 128] for n in range(2)], axis=1
        )

    def forward(half):
        def step(i):
            rows = block(i, TILE)
            column = columns(i)
            for imgs in range(half * 512, half * 512 + 512, 256):
                cols = slice(imgs, imgs + 256)
                cosine = lax.dot_general(
                    nh[rows, :], uh[cols, :], (((1,), (1,)), ((), ())), preferred_element_type=F32
                )
                match = matches(column, imgs)
                scale = LOGIT_SCALE * LOG2E
                shift = jnp.where(match, scale * (1.0 + COS_MARGIN), scale)
                exp_terms = jnp.exp2(scale * cosine - shift)
                hit = jnp.where(match, cosine - COS_MARGIN, 0.0)
                sums[0, :, cols] += jnp.sum(exp_terms.reshape(TILE // 8, 8, 256), axis=0)
                sums[1, :, cols] += jnp.sum(hit.reshape(TILE // 8, 8, 256), axis=0)
                expt[rows, cols] = exp_terms.astype(BF16)

        return step

    def slopes(i):
        rows = block(i, 128)
        for k in range(6):
            v = hid[k, rows, :].astype(F32)
            half, t = gelu_parts(v)
            inner = ROOT * (1.0 + 3.0 * CUBIC * (v * v))
            slope[rows, k * 128 : (k + 1) * 128] = half + 0.5 * v * ((1.0 - t * t) * inner)
            act_t[k * 128 : (k + 1) * 128, rows] = jnp.transpose(v * half).astype(BF16)

    found = ([], [])

    def totals(half):
        cols = slice(half * 512, half * 512 + 512)
        pair = jnp.concatenate(
            [
                jnp.sum(sums[0, :, cols], axis=0, keepdims=True),
                jnp.sum(sums[1, :, cols], axis=0, keepdims=True) * LOGIT_SCALE,
            ],
            axis=0,
        )
        return pair_sums(
            place, pair, got.at[half], pair_send.at[half], pair_recv.at[half], started, found[half]
        )

    def settle(half):
        total, target = found[half][0][0:1, :], found[half][0][1:2, :]
        part = jnp.sum(LOGIT_SCALE + jnp.log(total) - target, axis=1, keepdims=True) * (1.0 / IMAGES)
        loss[...] = part if half == 0 else loss[...] + part
        sums[0, 0:1, half * 512 : half * 512 + 512] = FACTOR / total
        gut[...] = jnp.zeros_like(gut)

    def backward(half):
        def step(i):
            rows = block(i, TILE)
            column = columns(i)
            for part in range(0, 512, 256):
                imgs = half * 512 + part
                cols = slice(imgs, imgs + 256)
                match = matches(column, imgs)
                coeff = expt[rows, cols].astype(F32) * sums[0, 0:1, cols] - jnp.where(match, FACTOR, 0.0)
                coeff = coeff.astype(BF16)
                expt[rows, cols] = coeff
                gut[:, part : part + 256] += jnp.dot(nht[:, rows], coeff, preferred_element_type=F32)

        return step

    def split(half):
        acc, s0 = two[half][0], two[half][1]

        def step(i):
            rows = block(i, 128)
            for g in range(2):
                mine = block(place.core * 2 + g, 128)
                theirs = block((1 - place.core) * 2 + g, 128)
                acc[g, rows, :] = jnp.transpose(gut[mine, rows])
                s0[g, rows, :] = jnp.transpose(gut[theirs, rows])

        each(4, step)
        return sum_everywhere(place, half, 2, two[half], gu, started)

    done = [0]

    def centre_grads(count):
        def step(i):
            rows = block(i, TILE)
            grad_normed = jnp.dot(expt[rows, :], uh[...], preferred_element_type=F32)
            cen = centres[rows, :].astype(F32)
            inv = lax.rsqrt(jnp.sum(cen * cen, axis=1, keepdims=True) + NORM_EPSILON)
            normed = cen * inv
            along = jnp.sum(grad_normed * normed, axis=1, keepdims=True)
            nh[rows, :] = (inv * (grad_normed - normed * along)).astype(BF16)
            pltpu.make_async_copy(nh.at[rows], grad_centres.at[rows], out_sem.at[i]).start()

        each(count, step, done[0])
        done[0] += count

    def finish(half):
        def step(i):
            rows = block(i, 256)
            g = jnp.concatenate([gu[k, rows, :] for k in range(4)], axis=1).astype(F32)
            u = unit[rows, :]
            along = jnp.sum(g * u, axis=1, keepdims=True)
            grad_embed = (inv_embed[rows, :] * (g - u * along)).astype(BF16)
            ge[rows, :] = grad_embed
            grad_act = lax.dot_general(
                grad_embed, second[...], (((1,), (1,)), ((), ())), preferred_element_type=F32
            )
            act[rows, :] = (grad_act * slope[rows, :]).astype(BF16)

        each(2, step, 2 * half)
        rows = pl.ds(half * 512, 512)
        leave(act.at[rows], gh_hbm.at[rows])
        leave(ge.at[rows], ge_hbm.at[rows])

    def go(steps):
        next(steps, None)

    each(CENTRES // 128, normalise)
    loads[2].wait()
    a1 = product(0)
    go(a1)
    each(4, turn)
    go(a1)
    go(a1)
    go(a1)
    b1 = product(1)
    go(b1)
    each(4, turn, 4)
    leave(turned, turned_hbm)
    go(b1)
    go(a1)
    go(a1)
    go(b1)
    go(a1)
    go(b1)
    loads[3].wait()
    go(a1)
    each(2, embed)
    step = forward(0)
    each(6, step)
    go(b1)
    each(6, step, 6)
    go(b1)
    each(7, step, 12)
    ta = totals(0)
    go(ta)
    go(b1)
    each(2, slopes)
    go(ta)
    go(b1)
    each(2, embed, 2)
    step = forward(1)
    each(6, step)
    go(ta)
    each(6, step, 6)
    go(ta)
    each(7, step, 12)
    tb = totals(1)
    go(tb)
    each(1, slopes, 2)
    go(ta)
    settle(0)
    step = backward(0)
    each(5, step)
    go(tb)
    each(7, step, 5)
    go(tb)
    each(7, step, 12)
    a2 = split(0)
    go(a2)
    each(1, slopes, 3)
    go(tb)
    go(a2)
    each(4, slopes, 4)
    leave(act_t, act_t_hbm)
    go(tb)
    settle(1)
    step = backward(1)
    each(6, step)
    go(a2)
    each(7, step, 6)
    go(a2)
    each(6, step, 13)
    b2 = split(1)
    go(b2)
    go(a2)
    centre_grads(1)
    go(b2)
    centre_grads(4)
    go(a2)
    centre_grads(3)
    go(b2)
    go(a2)
    centre_grads(3)
    go(b2)
    go(a2)
    finish(0)
    centre_grads(2)
    go(b2)
    centre_grads(3)
    go(b2)
    centre_grads(3)
    go(b2)
    go(b2)
    finish(1)
    def drain(i):
        rows = block(i, TILE)
        pltpu.make_async_copy(nh.at[rows], grad_centres.at[rows], out_sem.at[i]).wait()

    each(CENTRES // TILE, drain)
    for copy in leaving:
        copy.wait()
    for half in range(2):
        for d in range(1, 8):
            copies[half][d].wait_send()
    for copy in started:
        copy.wait_send()


def last_kernel(
    turned_hbm, gh_hbm, act_t_hbm, ge_hbm, centres_hbm, loss_in,
    loss, grad_first, grad_second, grad_centres,
    turned, gh, act_t, ge, held, first, second, sem, in_sem, out_sem,
):
    sources = ((turned_hbm, turned), (gh_hbm, gh), (act_t_hbm, act_t), (ge_hbm, ge))
    loads = [pltpu.make_async_copy(src, dst, sem.at[i]) for i, (src, dst) in enumerate(sources)]
    count = 8
    size = CENTRES // count
    parts = [pl.ds(k * size, size) for k in range(count)]
    arrive = [pltpu.make_async_copy(centres_hbm.at[p], held.at[p], in_sem.at[k]) for k, p in enumerate(parts)]
    depart = [pltpu.make_async_copy(held.at[p], grad_centres.at[p], out_sem.at[k]) for k, p in enumerate(parts)]
    for load in loads[:2] + arrive + loads[2:]:
        load.start()
    loss[...] = loss_in[...]
    loads[0].wait()
    loads[1].wait()
    out = []

    def pass_on(lo, hi):
        for k in range(lo, hi):
            arrive[k].wait()
            depart[k].start()

    for n in range(3):
        rows = pl.ds(n * 288, 288)
        first[rows, :] = jnp.dot(turned[rows, :], gh[...], preferred_element_type=F32).astype(BF16)
        out.append(pltpu.make_async_copy(first.at[rows], grad_first.at[rows], sem.at[4 + n]))
        out[-1].start()
        pass_on(2 * n, 2 * n + 2)
    pass_on(6, 8)
    loads[2].wait()
    loads[3].wait()
    for n in range(3):
        rows = pl.ds(n * 256, 256)
        second[rows, :] = jnp.dot(act_t[rows, :], ge[...], preferred_element_type=F32).astype(BF16)
        out.append(pltpu.make_async_copy(second.at[rows], grad_second.at[rows], sem.at[7 + n]))
        out[-1].start()
    for copy in out + depart:
        copy.wait()


def shards(features, first_weight, second_weight, centres, active, labels):
    in_place = pl.BlockSpec(memory_space=pl.ANY)
    near = pl.BlockSpec(memory_space=pltpu.VMEM)
    dma = pltpu.SemaphoreType.DMA
    loss, turned, gh, act_t, ge, grads = pl.pallas_call(
        step_kernel,
        out_shape=(
            jax.ShapeDtypeStruct((1, 1), F32),
            jax.ShapeDtypeStruct((BLOCK, IMAGES), BF16),
            jax.ShapeDtypeStruct((IMAGES, HIDDEN), BF16),
            jax.ShapeDtypeStruct((HIDDEN, IMAGES), BF16),
            jax.ShapeDtypeStruct((IMAGES, EMBED), BF16),
            jax.ShapeDtypeStruct((CENTRES, EMBED), BF16),
        ),
        in_specs=[in_place] * 4 + [near] * 2,
        out_specs=(near,) + (in_place,) * 5,
        scratch_shapes=[
            pltpu.VMEM((128, 8 * BLOCK), BF16),
            pltpu.VMEM((BLOCK, HIDDEN), BF16),
            pltpu.VMEM((HIDDEN, EMBED), BF16),
            pltpu.VMEM((CENTRES, EMBED), BF16),
            pltpu.VMEM((8, 128, BLOCK), BF16),
            pltpu.VMEM((IMAGES, BLOCK), BF16),
            pltpu.VMEM((BLOCK, IMAGES), BF16),
            pltpu.VMEM((CENTRES, EMBED), BF16),
            pltpu.VMEM((EMBED, CENTRES), BF16),
            pltpu.VMEM((CENTRES, IMAGES), BF16),
            pltpu.VMEM((6, IMAGES, 128), BF16),
            pltpu.VMEM((IMAGES, HIDDEN), BF16),
            pltpu.VMEM((HIDDEN, IMAGES), BF16),
            pltpu.VMEM((IMAGES, HIDDEN), F32),
            pltpu.VMEM((IMAGES, EMBED), F32),
            pltpu.VMEM((IMAGES, EMBED), BF16),
            pltpu.VMEM((IMAGES, 1), F32),
            pltpu.VMEM((EMBED, 512), F32),
            pltpu.VMEM((4, IMAGES, 128), BF16),
            pltpu.VMEM((IMAGES, EMBED), BF16),
            pltpu.VMEM((2, 8, IMAGES), F32),
            pltpu.VMEM((2, 4, 4, 2, 512), F32),
            pltpu.VMEM((1, IMAGES), jnp.int32),
            dma((10,)),
            dma((CENTRES // TILE,)),
            dma((2, 8)),
            dma((2, 8)),
            dma((2, 4, 3)),
            dma((2, 4, 3)),
        ]
        + sum_scratch(3) * 2
        + sum_scratch(2) * 2,
        compiler_params=pltpu.CompilerParams(
            collective_id=0, has_side_effects=True, vmem_limit_bytes=67043328
        ),
    )(
        features,
        first_weight,
        second_weight,
        centres,
        active.reshape(1, CENTRES),
        labels.reshape(1, IMAGES),
    )
    loss, grad_first, grad_second, grad_centres = pl.pallas_call(
        last_kernel,
        out_shape=(
            jax.ShapeDtypeStruct((1, 1), F32),
            jax.ShapeDtypeStruct((BLOCK, HIDDEN), BF16),
            jax.ShapeDtypeStruct((HIDDEN, EMBED), BF16),
            jax.ShapeDtypeStruct((CENTRES, EMBED), BF16),
        ),
        in_specs=[in_place] * 5 + [near],
        out_specs=(near,) + (in_place,) * 3,
        scratch_shapes=[
            pltpu.VMEM((BLOCK, IMAGES), BF16),
            pltpu.VMEM((IMAGES, HIDDEN), BF16),
            pltpu.VMEM((HIDDEN, IMAGES), BF16),
            pltpu.VMEM((IMAGES, EMBED), BF16),
            pltpu.VMEM((CENTRES, EMBED), BF16),
            pltpu.VMEM((BLOCK, HIDDEN), BF16),
            pltpu.VMEM((HIDDEN, EMBED), BF16),
            dma((10,)),
            dma((8,)),
            dma((8,)),
        ],
        compiler_params=pltpu.CompilerParams(vmem_limit_bytes=60000000),
    )(turned, gh, act_t, ge, grads, loss)
    return loss.reshape(()), grad_first, grad_second, grad_centres


def solution(mesh):
    placed = (
        P("gx", "gy"),
        P(("gy", "gx"), None),
        P(),
        P(("gx", "gy"), None),
        P(("gx", "gy")),
        P(),
    )
    return jax.shard_map(
        shards,
        mesh=mesh,
        in_specs=placed,
        out_specs=(P(), P(("gy", "gx"), None), P(), P(("gx", "gy"), None)),
        check_vma=False,
    )
```

```python
import jax
import jax.numpy as jnp
from jax import lax
from jax.experimental import pallas as pl
from jax.experimental.pallas import tpu as pltpu
from jax.sharding import PartitionSpec as P

CLS_DEV = 16128
LOGIT_SCALE = 64.0
COS_MARGIN = 0.4
NORM_EPSILON = 1e-06

MESH = pl.DeviceIdType.MESH
BF16 = jnp.bfloat16
F32 = jnp.float32
IMAGES = 1024
HIDDEN = 768
EMBED = 512
BLOCK = 864
CENTRES = 4864
FACTOR = LOGIT_SCALE / IMAGES
LOG2E = 1.4426950408889634
ROOT = 0.7978845608028654
CUBIC = 0.044715
ORDERS = (
    (("x", "z", "y"), ("z", "x", "y"), ("x", "z", "y")),
    (("x", "y", "z"), ("y", "z", "x"), ("z", "x", "y")),
)
TILE = 256


class Place:
    def __init__(self):
        gx, gy = lax.axis_index("gx"), lax.axis_index("gy")
        self.gx, self.gy = gx, gy
        self.core = lax.rem(gx, 2)
        self.pos = {"y": lax.div(gx, 2), "z": lax.div(gy, 4), "x": lax.rem(gy, 4)}

    def peer(self, axis, d):
        q = lax.rem(self.pos[axis] + d, 4)
        if axis == "y":
            return (q * 2 + self.core, self.gy)
        if axis == "z":
            return (self.gx, q * 4 + self.pos["x"])
        return (self.gx, self.pos["z"] * 4 + q)

    def partner(self):
        return (self.gx + 1 - 2 * self.core, self.gy)

    def row(self, d):
        return (lax.rem(self.gx + d, 8), self.gy)

    def greet(self, meanwhile):
        barrier = pltpu.get_barrier_semaphore()
        devices = [self.peer(axis, d) for axis in ("x", "z") for d in (1, 2, 3)]
        devices += [self.row(d) for d in range(1, 8)]
        for device in devices:
            pl.semaphore_signal(barrier, inc=1, device_id=device, device_id_type=MESH)
        meanwhile()
        pl.semaphore_wait(barrier, len(devices))


def remote(src, dst, send, recv, device):
    return pltpu.make_async_remote_copy(
        src_ref=src, dst_ref=dst, send_sem=send, recv_sem=recv, device_id=device, device_id_type=MESH
    )


def block(index, size):
    return pl.ds(pl.multiple_of(index * size, size), size)


def each(count, body, start=0):
    def step(i, carry):
        body(i)
        return carry

    lax.fori_loop(start, start + count, step, 0)


def sum_scratch(groups):
    return [
        pltpu.VMEM((groups, 512, 128), F32),
        pltpu.VMEM((groups, 512, 128), F32),
        pltpu.VMEM((groups, 512, 128), F32),
        pltpu.VMEM((groups, 512, 128), BF16),
        pltpu.VMEM((groups, 3, 128, 128), BF16),
        pltpu.VMEM((groups, 128, 128), F32),
        pltpu.VMEM((groups, 3, 32, 128), F32),
        pltpu.VMEM((groups, 4, 32, 128), F32),
        pltpu.SemaphoreType.DMA((groups, 7, 3)),
        pltpu.SemaphoreType.DMA((groups, 7, 3)),
    ]


def sum_everywhere(place, half, groups, orders, bufs, out, started):
    acc, s0, r0, s1, r1, acc2, r2, x3, send, recv = bufs
    core = place.core

    def go(src, dst, g, stage, k, device):
        copy = remote(src, dst, send.at[g, stage, k], recv.at[g, stage, k], device)
        copy.start()
        started.append(copy)
        return copy

    def scatter(g, stage, axis, sent, got, size):
        copies = []
        for d in (2, 1, 3):
            rows = block(lax.rem(place.pos[axis] + d, 4), size)
            copies.append(go(sent.at[g, rows], got.at[g, d - 1], g, stage, d - 1, place.peer(axis, d)))
        return copies

    def spread(g, stage, axis, base, size):
        part = out.at[core * groups + g, pl.ds(pl.multiple_of(base, size), size)]
        return [go(part, part, g, stage, d - 1, place.peer(axis, d)) for d in (2, 1, 3)]

    live = [go(s0.at[g], r0.at[g], g, 0, 0, place.partner()) for g in range(groups)]
    yield
    nxt = []
    for g in range(groups):
        live[g].wait_recv()

        def add(i, g=g):
            rows = block(i, 128)
            total = acc[g, rows, :] + r0[g, rows, :]
            acc[g, rows, :] = total
            s1[g, rows, :] = total.astype(BF16)

        each(4, add)
        nxt.append(scatter(g, 1, orders[g][0], s1, r1, 128))
    live, nxt = nxt, []
    yield
    for g in range(groups):
        for copy in live[g]:
            copy.wait_recv()
        own = block(place.pos[orders[g][0]], 128)
        acc2[g] = acc[g, own, :] + (r1[g, 0].astype(F32) + r1[g, 1].astype(F32) + r1[g, 2].astype(F32))
        nxt.append(scatter(g, 2, orders[g][1], acc2, r2, 32))
    live, nxt = nxt, []
    yield
    for g in range(groups):
        for copy in live[g]:
            copy.wait_recv()
        own = block(place.pos[orders[g][1]], 32)
        p = place.pos[orders[g][2]]
        x3[g, p] = acc2[g, own, :] + (r2[g, 0] + r2[g, 1] + r2[g, 2])
        slot = x3.at[g, p]
        nxt.append([go(slot, slot, g, 3, d - 1, place.peer(orders[g][2], d)) for d in (2, 1, 3)])
    live, nxt = nxt, []
    yield
    bases = []
    for g in range(groups):
        for copy in live[g]:
            copy.wait_recv()
        first = half * 512 + place.pos[orders[g][0]] * 128
        bases.append((first + place.pos[orders[g][1]] * 32, first))
        total = (x3[g, 0] + x3[g, 1]) + (x3[g, 2] + x3[g, 3])
        out[core * groups + g, pl.ds(pl.multiple_of(bases[g][0], 32), 32), :] = total.astype(BF16)
        nxt.append(spread(g, 4, orders[g][1], bases[g][0], 32))
    live, nxt = nxt, []
    yield
    for g in range(groups):
        for copy in live[g]:
            copy.wait_recv()
        nxt.append(spread(g, 5, orders[g][0], bases[g][1], 128))
    live, last = nxt, []
    yield
    for g in range(groups):
        for copy in live[g]:
            copy.wait_recv()
        whole = out.at[core * groups + g, pl.ds(half * 512, 512)]
        last.append(go(whole, whole, g, 6, 0, place.partner()))
    yield
    for copy in last:
        copy.wait_recv()


def pair_sums(place, value, got, send, recv, started, keep):
    for stage, axis in enumerate(("core", "x", "y", "z")):
        p = place.core if axis == "core" else place.pos[axis]
        got[stage, p] = value
        copies = []
        for d in (1,) if axis == "core" else (2, 1, 3):
            device = place.partner() if axis == "core" else place.peer(axis, d)
            slot = got.at[stage, p]
            copies.append(remote(slot, slot, send.at[stage, d - 1], recv.at[stage, d - 1], device))
            copies[-1].start()
        yield
        for copy in copies:
            copy.wait_recv()
        started += copies
        value = got[stage, 0] + got[stage, 1]
        if axis != "core":
            value = value + (got[stage, 2] + got[stage, 3])
    keep.append(value)


def gelu_parts(v):
    t = jnp.tanh(ROOT * (v + CUBIC * (v * v * v)))
    return 0.5 * (1.0 + t), t


def step_kernel(
    features_hbm, weight_hbm, second_hbm, centres_hbm, active, labels,
    loss, turned_hbm, gh_hbm, act_t_hbm, ge_hbm, grad_centres,
    features, weight, second, centres, sends, blocks, turned, nh, nht, expt,
    hid, act, act_t, slope, unit, uh, inv_embed, gut, gu, ge,
    sums, got, places, held0, held1, pair0, pair1, local_sem, out_sem, a2a_send, a2a_recv, pair_send, pair_recv, *bufs,
):
    size = len(bufs) // 4
    one, two = (bufs[:size], bufs[size : 2 * size]), (bufs[2 * size : 3 * size], bufs[3 * size :])
    place = Place()
    me = place.gx
    device = me * 16 + place.gy
    started, leaving = [], []
    loads = [
        pltpu.make_async_copy(src, dst, local_sem.at[i])
        for i, (src, dst) in enumerate(
            ((features_hbm, features), (centres_hbm, centres), (weight_hbm, weight), (second_hbm, second))
        )
    ]

    def leave(src, dst):
        leaving.append(pltpu.make_async_copy(src, dst, local_sem.at[4 + len(leaving)]))
        leaving[-1].start()

    def prepare():
        for load in loads:
            load.start()
        loads[0].wait()
        for j in range(8):
            sends[j] = features[:, j * BLOCK : (j + 1) * BLOCK]

    place.greet(prepare)
    copies = ({}, {})
    def exchange(half):
        for d in (4, 5, 3, 2, 6, 7, 1):
            copies[half][d] = remote(
                sends.at[lax.rem(me + d, 8), pl.ds(half * 64, 64)],
                blocks.at[pl.ds(pl.multiple_of(half * 512 + me * 64, 64), 64)],
                a2a_send.at[half, d],
                a2a_recv.at[half, d],
                place.row(d),
            )
            copies[half][d].start()

    exchange(0)
    for half in range(2):
        blocks[pl.ds(pl.multiple_of(half * 512 + me * 64, 64), 64), :] = sends[me, half * 64 : half * 64 + 64, :]
        for j in range(8):
            spot = half * 512 + j * 64
            places[:, spot : spot + 64] = labels[:, j * 128 + half * 64 : j * 128 + half * 64 + 64]
    sums[...] = jnp.zeros_like(sums)
    loads[1].wait()

    def normalise(i):
        rows = block(i, 128)
        cen = centres[rows, :].astype(F32)
        normed = cen * lax.rsqrt(jnp.sum(cen * cen, axis=1, keepdims=True) + NORM_EPSILON)
        nh[rows, :] = normed.astype(BF16)
        nht[:, rows] = jnp.transpose(normed).astype(BF16)

    def product(half):
        acc, s0 = one[half][0], one[half][1]
        mine = pl.ds(pl.multiple_of(place.core * 384, 128), 384)
        theirs = pl.ds(pl.multiple_of((1 - place.core) * 384, 128), 384)
        for d in range(1, 8):
            copies[half][d].wait_recv()

        def step(i):
            rows = block(i, 256)
            piece = blocks[pl.ds(pl.multiple_of(half * 512 + i * 256, 256), 256), :]
            other = jnp.dot(piece, weight[:, theirs], preferred_element_type=F32)
            own = jnp.dot(piece, weight[:, mine], preferred_element_type=F32)
            for g in range(3):
                acc[g, rows, :] = own[:, g * 128 : (g + 1) * 128]
                s0[g, rows, :] = other[:, g * 128 : (g + 1) * 128]

        each(2, step)
        return sum_everywhere(place, half, 3, ORDERS[half], one[half], hid, started)

    def turn(i):
        rows = block(i, 128)
        for k in range(0, BLOCK, 128):
            top = min(k + 128, BLOCK)
            turned[k:top, rows] = jnp.transpose(blocks[rows, k:top].astype(F32)).astype(BF16)

    def embed(i):
        rows = block(i, 256)
        for k in range(6):
            v = hid[k, rows, :].astype(F32)
            act[rows, k * 128 : (k + 1) * 128] = (v * gelu_parts(v)[0]).astype(BF16)
        emb = jnp.dot(act[rows, :], second[...], preferred_element_type=F32)
        inv = lax.rsqrt(jnp.sum(emb * emb, axis=1, keepdims=True) + NORM_EPSILON)
        inv_embed[rows, :] = inv
        u = emb * inv
        unit[rows, :] = u
        uh[rows, :] = u.astype(BF16)

    def columns(i):
        parts = []
        for k in range(TILE // 128):
            row = active[:, block(i * (TILE // 128) + k, 128)] + device * CLS_DEV
            parts.append(jnp.transpose(jnp.broadcast_to(row, (128, 128))))
        return jnp.concatenate(parts, axis=0)

    def cosines(half, i, held):
        held[...] = lax.dot_general(
            nh[block(i, TILE), :],
            uh[half * 512 : half * 512 + 512, :],
            (((1,), (1,)), ((), ())),
            preferred_element_type=F32,
        )

    def terms(half, i, held):
        rows = block(i, TILE)
        column = columns(i)
        for part in range(0, 512, 128):
            cols = slice(half * 512 + part, half * 512 + part + 128)
            cosine = held[:, part : part + 128]
            match = column == places[:, cols]
            scale = LOGIT_SCALE * LOG2E
            exp_terms = jnp.exp2(scale * cosine - jnp.where(match, scale * (1.0 + COS_MARGIN), scale))
            hit = jnp.where(match, cosine - COS_MARGIN, 0.0)
            sums[0, :, cols] += jnp.sum(exp_terms.reshape(TILE // 8, 8, 128), axis=0)
            sums[1, :, cols] += jnp.sum(hit.reshape(TILE // 8, 8, 128), axis=0)
            expt[rows, cols] = exp_terms.astype(BF16)

    def forward(half):
        cosines(half, 0, held0)

        def step(i):
            cosines(half, 2 * i + 1, held1)
            terms(half, 2 * i, held0)
            cosines(half, 2 * i + 2, held0)
            terms(half, 2 * i + 1, held1)

        return step

    def slopes(i):
        rows = block(i, 128)
        for k in range(6):
            v = hid[k, rows, :].astype(F32)
            half, t = gelu_parts(v)
            inner = ROOT * (1.0 + 3.0 * CUBIC * (v * v))
            slope[rows, k * 128 : (k + 1) * 128] = half + 0.5 * v * ((1.0 - t * t) * inner)
            act_t[k * 128 : (k + 1) * 128, rows] = jnp.transpose(v * half).astype(BF16)

    found = ([], [])

    def totals(half):
        cols = slice(half * 512, half * 512 + 512)
        pair = jnp.concatenate(
            [
                jnp.sum(sums[0, :, cols], axis=0, keepdims=True),
                jnp.sum(sums[1, :, cols], axis=0, keepdims=True) * LOGIT_SCALE,
            ],
            axis=0,
        )
        return pair_sums(
            place, pair, got.at[half], pair_send.at[half], pair_recv.at[half], started, found[half]
        )

    def settle(half):
        total, target = found[half][0][0:1, :], found[half][0][1:2, :]
        part = jnp.sum(LOGIT_SCALE + jnp.log(total) - target, axis=1, keepdims=True) * (1.0 / IMAGES)
        loss[...] = part if half == 0 else loss[...] + part
        sums[0, 0:1, half * 512 : half * 512 + 512] = FACTOR / total
        gut[...] = jnp.zeros_like(gut)

    def coeffs(half, start, held, tiles=2):
        for k in range(tiles):
            i = start + k
            rows = block(i, TILE)
            column = columns(i)
            for part in range(0, 512, 128):
                cols = slice(half * 512 + part, half * 512 + part + 128)
                match = column == places[:, cols]
                coeff = expt[rows, cols].astype(F32) * sums[0, 0:1, cols] - jnp.where(match, FACTOR, 0.0)
                coeff = coeff.astype(BF16)
                expt[rows, cols] = coeff
                held[k * TILE : (k + 1) * TILE, part : part + 128] = coeff

    def weigh(start, held, tiles=2):
        cols = pl.ds(pl.multiple_of(start * TILE, TILE), tiles * TILE)
        gut[...] += jnp.dot(nht[:, cols], held[: tiles * TILE, :], preferred_element_type=F32)

    def backward(half):
        coeffs(half, 0, pair0)

        def step(i):
            weigh(4 * i, pair0)
            coeffs(half, 4 * i + 2, pair1)
            weigh(4 * i + 2, pair1)
            coeffs(half, 4 * i + 4, pair0)

        return step

    def backward_end(half):
        weigh(16, pair0)
        coeffs(half, 18, pair1, 1)
        weigh(18, pair1, 1)

    def split(half):
        acc, s0 = two[half][0], two[half][1]

        def step(i):
            rows = block(i, 128)
            for g in range(2):
                mine = block(place.core * 2 + g, 128)
                theirs = block((1 - place.core) * 2 + g, 128)
                acc[g, rows, :] = jnp.transpose(gut[mine, rows])
                s0[g, rows, :] = jnp.transpose(gut[theirs, rows])

        each(4, step)
        return sum_everywhere(place, half, 2, ORDERS[1], two[half], gu, started)

    done = [0]

    def pull(i, held):
        held[...] = jnp.dot(expt[block(i, TILE), :], uh[...], preferred_element_type=F32)

    def centre(i, held):
        rows = block(i, TILE)
        cen = centres[rows, :].astype(F32)
        inv = lax.rsqrt(jnp.sum(cen * cen, axis=1, keepdims=True) + NORM_EPSILON)
        normed = cen * inv
        grad_normed = held[...]
        along = jnp.sum(grad_normed * normed, axis=1, keepdims=True)
        nh[rows, :] = (inv * (grad_normed - normed * along)).astype(BF16)
        pltpu.make_async_copy(nh.at[rows], grad_centres.at[rows], out_sem.at[i]).start()

    def centre_grads(count):
        if done[0] == 0:
            pull(0, held0)

        def step(i):
            pull(2 * i + 1, held1)
            centre(2 * i, held0)
            pull(2 * i + 2, held0)
            centre(2 * i + 1, held1)

        each(count, step, done[0])
        done[0] += count
        if done[0] == 9:
            centre(18, held0)

    def finish(half):
        def step(i):
            rows = block(i, 256)
            g = jnp.concatenate([gu[k, rows, :] for k in range(4)], axis=1).astype(F32)
            u = unit[rows, :]
            along = jnp.sum(g * u, axis=1, keepdims=True)
            grad_embed = (inv_embed[rows, :] * (g - u * along)).astype(BF16)
            ge[rows, :] = grad_embed
            grad_act = lax.dot_general(
                grad_embed, second[...], (((1,), (1,)), ((), ())), preferred_element_type=F32
            )
            act[rows, :] = (grad_act * slope[rows, :]).astype(BF16)

        each(2, step, 2 * half)
        rows = pl.ds(half * 512, 512)
        leave(act.at[rows], gh_hbm.at[rows])
        leave(ge.at[rows], ge_hbm.at[rows])

    def go(steps):
        next(steps, None)

    each(24, normalise)
    exchange(1)
    each(CENTRES // 128 - 24, normalise, 24)
    loads[2].wait()
    a1 = product(0)
    go(a1)
    each(4, turn)
    go(a1)
    go(a1)
    go(a1)
    b1 = product(1)
    go(b1)
    each(4, turn, 4)
    leave(turned, turned_hbm)
    go(b1)
    go(a1)
    go(a1)
    go(b1)
    go(a1)
    go(b1)
    loads[3].wait()
    go(a1)
    each(2, embed)
    step = forward(0)
    each(3, step)
    go(b1)
    each(3, step, 3)
    go(b1)
    each(3, step, 6)
    terms(0, 18, held0)
    ta = totals(0)
    go(ta)
    go(b1)
    each(2, slopes)
    go(ta)
    go(b1)
    each(2, embed, 2)
    step = forward(1)
    each(4, step)
    go(ta)
    each(5, step, 4)
    terms(1, 18, held0)
    go(ta)
    tb = totals(1)
    go(tb)
    each(2, slopes, 2)
    go(ta)
    go(tb)
    settle(0)
    step = backward(0)
    each(2, step)
    go(tb)
    each(2, step, 2)
    backward_end(0)
    a2 = split(0)
    go(a2)
    each(1, slopes, 4)
    go(tb)
    go(a2)
    each(3, slopes, 5)
    leave(act_t, act_t_hbm)
    go(tb)
    settle(1)
    step = backward(1)
    each(2, step)
    go(a2)
    each(2, step, 2)
    backward_end(1)
    go(a2)
    b2 = split(1)
    go(b2)
    centre_grads(1)
    go(b2)
    go(a2)
    centre_grads(2)
    go(b2)
    go(a2)
    centre_grads(2)
    go(b2)
    go(a2)
    go(b2)
    centre_grads(1)
    go(a2)
    finish(0)
    centre_grads(1)
    go(b2)
    centre_grads(2)
    go(b2)
    go(b2)
    finish(1)
    def drain(i):
        rows = block(i, TILE)
        pltpu.make_async_copy(nh.at[rows], grad_centres.at[rows], out_sem.at[i]).wait()

    each(CENTRES // TILE, drain)
    for copy in leaving:
        copy.wait()
    for half in range(2):
        for d in range(1, 8):
            copies[half][d].wait_send()
    for copy in started:
        copy.wait_send()


def last_kernel(
    turned_hbm, gh_hbm, act_t_hbm, ge_hbm, centres_hbm, loss_in,
    loss, grad_first, grad_second, grad_centres,
    turned, gh, act_t, ge, held, first, second, sem, in_sem, out_sem,
):
    sources = ((turned_hbm, turned), (gh_hbm, gh), (act_t_hbm, act_t), (ge_hbm, ge))
    loads = [pltpu.make_async_copy(src, dst, sem.at[i]) for i, (src, dst) in enumerate(sources)]
    count = 8
    size = CENTRES // count
    parts = [pl.ds(k * size, size) for k in range(count)]
    arrive = [pltpu.make_async_copy(centres_hbm.at[p], held.at[p], in_sem.at[k]) for k, p in enumerate(parts)]
    depart = [pltpu.make_async_copy(held.at[p], grad_centres.at[p], out_sem.at[k]) for k, p in enumerate(parts)]
    for load in loads[:2] + arrive + loads[2:]:
        load.start()
    loss[...] = loss_in[...]
    loads[0].wait()
    loads[1].wait()
    out = []

    def pass_on(lo, hi):
        for k in range(lo, hi):
            arrive[k].wait()
            depart[k].start()

    for n in range(3):
        rows = pl.ds(n * 288, 288)
        first[rows, :] = jnp.dot(turned[rows, :], gh[...], preferred_element_type=F32).astype(BF16)
        out.append(pltpu.make_async_copy(first.at[rows], grad_first.at[rows], sem.at[4 + n]))
        out[-1].start()
        pass_on(2 * n, 2 * n + 2)
    pass_on(6, 8)
    loads[2].wait()
    loads[3].wait()
    for n in range(3):
        rows = pl.ds(n * 256, 256)
        second[rows, :] = jnp.dot(act_t[rows, :], ge[...], preferred_element_type=F32).astype(BF16)
        out.append(pltpu.make_async_copy(second.at[rows], grad_second.at[rows], sem.at[7 + n]))
        out[-1].start()
    for copy in out + depart:
        copy.wait()


def shards(features, first_weight, second_weight, centres, active, labels):
    in_place = pl.BlockSpec(memory_space=pl.ANY)
    near = pl.BlockSpec(memory_space=pltpu.VMEM)
    dma = pltpu.SemaphoreType.DMA
    loss, turned, gh, act_t, ge, grads = pl.pallas_call(
        step_kernel,
        out_shape=(
            jax.ShapeDtypeStruct((1, 1), F32),
            jax.ShapeDtypeStruct((BLOCK, IMAGES), BF16),
            jax.ShapeDtypeStruct((IMAGES, HIDDEN), BF16),
            jax.ShapeDtypeStruct((HIDDEN, IMAGES), BF16),
            jax.ShapeDtypeStruct((IMAGES, EMBED), BF16),
            jax.ShapeDtypeStruct((CENTRES, EMBED), BF16),
        ),
        in_specs=[in_place] * 4 + [near] * 2,
        out_specs=(near,) + (in_place,) * 5,
        scratch_shapes=[
            pltpu.VMEM((128, 8 * BLOCK), BF16),
            pltpu.VMEM((BLOCK, HIDDEN), BF16),
            pltpu.VMEM((HIDDEN, EMBED), BF16),
            pltpu.VMEM((CENTRES, EMBED), BF16),
            pltpu.VMEM((8, 128, BLOCK), BF16),
            pltpu.VMEM((IMAGES, BLOCK), BF16),
            pltpu.VMEM((BLOCK, IMAGES), BF16),
            pltpu.VMEM((CENTRES, EMBED), BF16),
            pltpu.VMEM((EMBED, CENTRES), BF16),
            pltpu.VMEM((CENTRES, IMAGES), BF16),
            pltpu.VMEM((6, IMAGES, 128), BF16),
            pltpu.VMEM((IMAGES, HIDDEN), BF16),
            pltpu.VMEM((HIDDEN, IMAGES), BF16),
            pltpu.VMEM((IMAGES, HIDDEN), F32),
            pltpu.VMEM((IMAGES, EMBED), F32),
            pltpu.VMEM((IMAGES, EMBED), BF16),
            pltpu.VMEM((IMAGES, 1), F32),
            pltpu.VMEM((EMBED, 512), F32),
            pltpu.VMEM((4, IMAGES, 128), BF16),
            pltpu.VMEM((IMAGES, EMBED), BF16),
            pltpu.VMEM((2, 8, IMAGES), F32),
            pltpu.VMEM((2, 4, 4, 2, 512), F32),
            pltpu.VMEM((1, IMAGES), jnp.int32),
            pltpu.VMEM((TILE, 512), F32),
            pltpu.VMEM((TILE, 512), F32),
            pltpu.VMEM((2 * TILE, 512), BF16),
            pltpu.VMEM((2 * TILE, 512), BF16),
            dma((10,)),
            dma((CENTRES // TILE,)),
            dma((2, 8)),
            dma((2, 8)),
            dma((2, 4, 3)),
            dma((2, 4, 3)),
        ]
        + sum_scratch(3) * 2
        + sum_scratch(2) * 2,
        compiler_params=pltpu.CompilerParams(
            collective_id=0, has_side_effects=True, vmem_limit_bytes=67043328
        ),
    )(
        features,
        first_weight,
        second_weight,
        centres,
        active.reshape(1, CENTRES),
        labels.reshape(1, IMAGES),
    )
    loss, grad_first, grad_second, grad_centres = pl.pallas_call(
        last_kernel,
        out_shape=(
            jax.ShapeDtypeStruct((1, 1), F32),
            jax.ShapeDtypeStruct((BLOCK, HIDDEN), BF16),
            jax.ShapeDtypeStruct((HIDDEN, EMBED), BF16),
            jax.ShapeDtypeStruct((CENTRES, EMBED), BF16),
        ),
        in_specs=[in_place] * 5 + [near],
        out_specs=(near,) + (in_place,) * 3,
        scratch_shapes=[
            pltpu.VMEM((BLOCK, IMAGES), BF16),
            pltpu.VMEM((IMAGES, HIDDEN), BF16),
            pltpu.VMEM((HIDDEN, IMAGES), BF16),
            pltpu.VMEM((IMAGES, EMBED), BF16),
            pltpu.VMEM((CENTRES, EMBED), BF16),
            pltpu.VMEM((BLOCK, HIDDEN), BF16),
            pltpu.VMEM((HIDDEN, EMBED), BF16),
            dma((10,)),
            dma((8,)),
            dma((8,)),
        ],
        compiler_params=pltpu.CompilerParams(vmem_limit_bytes=60000000),
    )(turned, gh, act_t, ge, grads, loss)
    return loss.reshape(()), grad_first, grad_second, grad_centres


def solution(mesh):
    placed = (
        P("gx", "gy"),
        P(("gy", "gx"), None),
        P(),
        P(("gx", "gy"), None),
        P(("gx", "gy")),
        P(),
    )
    return jax.shard_map(
        shards,
        mesh=mesh,
        in_specs=placed,
        out_specs=(P(), P(("gy", "gx"), None), P(), P(("gx", "gy"), None)),
        check_vma=False,
    )
```

```python
import jax
import jax.numpy as jnp
import numpy as np
from jax import lax
from jax.experimental import pallas as pl
from jax.experimental.pallas import tpu as pltpu
from jax.sharding import PartitionSpec as P

CLS_DEV = 16128
LOGIT_SCALE = 64.0
COS_MARGIN = 0.4
NORM_EPSILON = 1e-06

MESH = pl.DeviceIdType.MESH
BF16 = jnp.bfloat16
F32 = jnp.float32
IMAGES = 1024
HIDDEN = 768
EMBED = 512
BLOCK = 864
CENTRES = 4864
FACTOR = LOGIT_SCALE / IMAGES
SCALE = float(np.float32(LOGIT_SCALE * 1.4426950408889634))
MARGIN = SCALE * COS_MARGIN
STEP = float(np.float32(SCALE + MARGIN) - np.float32(SCALE))
ROOT = 0.7978845608028654
CUBIC = 0.044715
ORDERS = (
    (("x", "z", "y"), ("z", "x", "y"), ("x", "z", "y")),
    (("x", "y", "z"), ("y", "z", "x"), ("z", "x", "y")),
)
TILE = 256
PARTS = 4
PART = IMAGES // PARTS
SHARE = 128 // PARTS


class Place:
    def __init__(self):
        gx, gy = lax.axis_index("gx"), lax.axis_index("gy")
        self.gx, self.gy = gx, gy
        self.core = lax.rem(gx, 2)
        self.pos = {"y": lax.div(gx, 2), "z": lax.div(gy, 4), "x": lax.rem(gy, 4)}

    def peer(self, axis, d):
        q = lax.rem(self.pos[axis] + d, 4)
        if axis == "y":
            return (q * 2 + self.core, self.gy)
        if axis == "z":
            return (self.gx, q * 4 + self.pos["x"])
        return (self.gx, self.pos["z"] * 4 + q)

    def partner(self):
        return (self.gx + 1 - 2 * self.core, self.gy)

    def row(self, d):
        return (lax.rem(self.gx + d, 8), self.gy)

    def greet(self, meanwhile):
        barrier = pltpu.get_barrier_semaphore()
        devices = [self.peer(axis, d) for axis in ("x", "z") for d in (1, 2, 3)]
        devices += [self.row(d) for d in range(1, 8)]
        for device in devices:
            pl.semaphore_signal(barrier, inc=1, device_id=device, device_id_type=MESH)
        meanwhile()
        pl.semaphore_wait(barrier, len(devices))


def remote(src, dst, send, recv, device):
    return pltpu.make_async_remote_copy(
        src_ref=src, dst_ref=dst, send_sem=send, recv_sem=recv, device_id=device, device_id_type=MESH
    )


def block(index, size):
    return pl.ds(pl.multiple_of(index * size, size), size)


def each(count, body, start=0):
    def step(i, carry):
        body(i)
        return carry

    lax.fori_loop(start, start + count, step, 0)


def sum_scratch(groups):
    return [
        pltpu.VMEM((groups, PART, 128), F32),
        pltpu.VMEM((groups, PART, 128), F32),
        pltpu.VMEM((groups, PART, 128), F32),
        pltpu.VMEM((groups, PART, 128), BF16),
        pltpu.VMEM((groups, 3, PART // 4, 128), BF16),
        pltpu.VMEM((groups, PART // 4, 128), F32),
        pltpu.VMEM((groups, 3, PART // 16, 128), F32),
        pltpu.VMEM((groups, 4, PART // 16, 128), F32),
        pltpu.SemaphoreType.DMA((7,)),
        pltpu.SemaphoreType.DMA((groups, 7)),
    ]


def landed(like, sem):
    pltpu.make_async_copy(like, like, sem).wait()


def sum_everywhere(place, part, groups, orders, bufs, out):
    acc, s0, r0, s1, r1, acc2, r2, x3, send, recv = bufs
    core = place.core
    like = (
        r0,
        r1,
        r2,
        x3.at[:, pl.ds(0, 3)],
        s1.at[:, pl.ds(0, 3 * (PART // 16))],
        r1,
        s1,
    )

    def go(src, dst, g, stage, device):
        remote(src, dst, send.at[stage], recv.at[g, stage], device).start()

    def scatter(g, stage, axis, sent, got, size):
        for d in (2, 1, 3):
            rows = block(lax.rem(place.pos[axis] + d, 4), size)
            go(sent.at[g, rows], got.at[g, d - 1], g, stage, place.peer(axis, d))

    def spread(g, stage, axis, base, size):
        piece = out.at[core * groups + g, pl.ds(pl.multiple_of(base, size), size)]
        for d in (2, 1, 3):
            go(piece, piece, g, stage, place.peer(axis, d))

    for g in range(groups):
        go(s0.at[g], r0.at[g], g, 0, place.partner())
    yield
    for g in range(groups):
        landed(like[0].at[g], recv.at[g, 0])

        def add(i, g=g):
            rows = block(i, 128)
            total = acc[g, rows, :] + r0[g, rows, :]
            acc[g, rows, :] = total
            s1[g, rows, :] = total.astype(BF16)

        each(2, add)
        scatter(g, 1, orders[g][0], s1, r1, PART // 4)
    landed(like[0], send.at[0])
    yield
    for g in range(groups):
        landed(like[1].at[g], recv.at[g, 1])
        own = block(place.pos[orders[g][0]], PART // 4)
        acc2[g] = acc[g, own, :] + (r1[g, 0].astype(F32) + r1[g, 1].astype(F32) + r1[g, 2].astype(F32))
        scatter(g, 2, orders[g][1], acc2, r2, PART // 16)
    landed(like[1], send.at[1])
    yield
    for g in range(groups):
        landed(like[2].at[g], recv.at[g, 2])
        own = block(place.pos[orders[g][1]], PART // 16)
        p = place.pos[orders[g][2]]
        x3[g, p] = acc2[g, own, :] + (r2[g, 0] + r2[g, 1] + r2[g, 2])
        slot = x3.at[g, p]
        for d in (2, 1, 3):
            go(slot, slot, g, 3, place.peer(orders[g][2], d))
    landed(like[2], send.at[2])
    yield
    bases = []
    for g in range(groups):
        landed(like[3].at[g], recv.at[g, 3])
        first = part * PART + place.pos[orders[g][0]] * (PART // 4)
        bases.append((first + place.pos[orders[g][1]] * (PART // 16), first))
        total = (x3[g, 0] + x3[g, 1]) + (x3[g, 2] + x3[g, 3])
        out[core * groups + g, pl.ds(pl.multiple_of(bases[g][0], PART // 16), PART // 16), :] = total.astype(BF16)
        spread(g, 4, orders[g][1], bases[g][0], PART // 16)
    landed(like[3], send.at[3])
    yield
    for g in range(groups):
        landed(like[4].at[g], recv.at[g, 4])
        spread(g, 5, orders[g][0], bases[g][1], PART // 4)
    landed(like[4], send.at[4])
    yield
    for g in range(groups):
        landed(like[5].at[g], recv.at[g, 5])
        whole = out.at[core * groups + g, pl.ds(part * PART, PART)]
        go(whole, whole, g, 6, place.partner())
    landed(like[5], send.at[5])
    yield
    for g in range(groups):
        landed(like[6].at[g], recv.at[g, 6])
    landed(like[6], send.at[6])


def pair_sums(place, value, got, send, recv, keep):
    for stage, axis in enumerate(("core", "x", "y", "z")):
        p = place.core if axis == "core" else place.pos[axis]
        got[stage, p] = value
        slot = got.at[stage, p]
        steps = (1,) if axis == "core" else (2, 1, 3)
        for d in steps:
            device = place.partner() if axis == "core" else place.peer(axis, d)
            remote(slot, slot, send.at[stage], recv.at[stage], device).start()
        yield
        like = got.at[stage, pl.ds(0, len(steps))]
        landed(like, recv.at[stage])
        value = got[stage, 0] + got[stage, 1]
        if axis != "core":
            value = value + (got[stage, 2] + got[stage, 3])
        landed(like, send.at[stage])
    keep.append(value)


def gelu_parts(v):
    t = jnp.tanh(ROOT * (v + CUBIC * (v * v * v)))
    return 0.5 * (1.0 + t), t


def step_kernel(
    features_hbm, weight_hbm, second_hbm, centres_hbm, active, labels,
    loss, grad_first, grad_second, grad_centres,
    features, weight, second, centres, sends, blocks, turned, nh, nht, expt,
    hid, act, act_t, slope, uh, inv_embed, gu, ge, first,
    sums, got, places, spots, where_found, held0, held1, wide0, wide1, pair0, pair1, local_sem, out_sem, a2a_send, a2a_recv, pair_send, pair_recv, *bufs,
):
    size = len(bufs) // (2 * PARTS)
    sets = [bufs[k * size : (k + 1) * size] for k in range(2 * PARTS)]
    one, two = sets[:PARTS], sets[PARTS:]
    place = Place()
    me = place.gx
    device = me * 16 + place.gy
    gut = held0
    loads = [
        pltpu.make_async_copy(src, dst, local_sem.at[i])
        for i, (src, dst) in enumerate(
            ((features_hbm, features), (centres_hbm, centres), (weight_hbm, weight), (second_hbm, second))
        )
    ]

    def prepare():
        for load in loads:
            load.start()
        loads[0].wait()
        for j in range(8):
            sends[j] = features[:, j * BLOCK : (j + 1) * BLOCK]

    place.greet(prepare)
    def exchange(part):
        for d in (4, 5, 3, 2, 6, 7, 1):
            remote(
                sends.at[lax.rem(me + d, 8), pl.ds(part * SHARE, SHARE)],
                blocks.at[pl.ds(pl.multiple_of(part * PART + me * SHARE, SHARE), SHARE)],
                a2a_send.at[part],
                a2a_recv.at[part],
                place.row(d),
            ).start()

    exchange(0)
    for part in range(PARTS):
        low = part * SHARE
        blocks[pl.ds(pl.multiple_of(part * PART + me * SHARE, SHARE), SHARE), :] = sends[me, low : low + SHARE, :]
        for j in range(8):
            spot = part * PART + j * SHARE
            places[:, spot : spot + SHARE] = labels[:, j * 128 + low : j * 128 + low + SHARE]
    sums[...] = jnp.zeros_like(sums)
    where_found[...] = jnp.full_like(where_found, -1.0)
    loads[1].wait()

    def normalise(i):
        rows = block(i, 128)
        cen = centres[rows, :].astype(F32)
        normed = cen * lax.rsqrt(jnp.sum(cen * cen, axis=1, keepdims=True) + NORM_EPSILON)
        nh[rows, :] = normed.astype(BF16)
        nht[:, rows] = jnp.transpose(normed).astype(BF16)

    def product(part):
        acc, s0 = one[part][0], one[part][1]
        mine = pl.ds(pl.multiple_of(place.core * 384, 128), 384)
        theirs = pl.ds(pl.multiple_of((1 - place.core) * 384, 128), 384)
        landed(blocks.at[pl.ds(0, 7 * SHARE)], a2a_recv.at[part])
        piece = blocks[part * PART : part * PART + PART, :]
        other = jnp.dot(piece, weight[:, theirs], preferred_element_type=F32)
        own = jnp.dot(piece, weight[:, mine], preferred_element_type=F32)
        for g in range(3):
            acc[g] = own[:, g * 128 : (g + 1) * 128]
            s0[g] = other[:, g * 128 : (g + 1) * 128]
        return sum_everywhere(place, part, 3, ORDERS[part // 3], one[part], hid)

    def turn(i):
        rows = block(i, 128)
        for k in range(0, BLOCK, 128):
            top = min(k + 128, BLOCK)
            turned[k:top, rows] = jnp.transpose(blocks[rows, k:top].astype(F32)).astype(BF16)

    def embed(i):
        rows = block(i, 256)
        for k in range(6):
            v = hid[k, rows, :].astype(F32)
            act[rows, k * 128 : (k + 1) * 128] = (v * gelu_parts(v)[0]).astype(BF16)
        emb = jnp.dot(act[rows, :], second[...], preferred_element_type=F32)
        inv = lax.rsqrt(jnp.sum(emb * emb, axis=1, keepdims=True) + NORM_EPSILON)
        inv_embed[rows, :] = inv
        u = emb * inv
        uh[rows, :] = u.astype(BF16)

    def locate(i):
        row = active[:, block(i, 128)] + device * CLS_DEV
        column = jnp.transpose(jnp.broadcast_to(row, (128, 128)))
        here = (lax.broadcasted_iota(jnp.int32, (128, 128), 0) + i * 128).astype(F32)
        for part in range(0, IMAGES, 128):
            cols = slice(part, part + 128)
            hit = jnp.where(column == places[:, cols], here, -1.0)
            best = jnp.max(hit.reshape(16, 8, 128), axis=0)
            where_found[:, cols] = jnp.maximum(where_found[:, cols], best)

    def columns(i):
        parts = []
        for k in range(TILE // 128):
            row = active[:, block(i * (TILE // 128) + k, 128)] + device * CLS_DEV
            parts.append(jnp.transpose(jnp.broadcast_to(row, (128, 128))))
        return jnp.concatenate(parts, axis=0)

    def matches(i, imgs):
        spot = spots[:, imgs : imgs + 128] - i * TILE
        return lax.broadcasted_iota(jnp.int32, (TILE, 128), 0) == spot

    def cosines(part, start, held, tiles=2):
        rows = pl.ds(pl.multiple_of(start * TILE, TILE), tiles * TILE)
        held[: tiles * TILE, :] = lax.dot_general(
            nh[rows, :],
            uh[part * PART : part * PART + PART, :],
            (((1,), (1,)), ((), ())),
            preferred_element_type=F32,
        )

    def terms(part, start, held, tiles=2):
        for k in range(tiles):
            i = start + k
            rows = block(i, TILE)
            for low in range(0, PART, 128):
                cols = slice(part * PART + low, part * PART + low + 128)
                cosine = held[k * TILE : (k + 1) * TILE, low : low + 128]
                shift = jnp.where(matches(i, part * PART + low), SCALE + MARGIN, SCALE)
                exp_terms = jnp.exp2(SCALE * cosine - shift)
                hit = (shift - SCALE) * cosine
                sums[0, :, cols] += jnp.sum(exp_terms.reshape(TILE // 8, 8, 128), axis=0)
                sums[1, :, cols] += jnp.sum(hit.reshape(TILE // 8, 8, 128), axis=0)
                expt[rows, cols] = exp_terms.astype(BF16)

    def forward(part, low, high):
        if low == 0:
            cosines(part, 0, held0)

        def step(i):
            cosines(part, 4 * i + 2, held1)
            terms(part, 4 * i, held0)
            cosines(part, 4 * i + 4, held0)
            terms(part, 4 * i + 2, held1)

        each(high - low, step, low)
        if high == 4:
            cosines(part, 18, held1, 1)
            terms(part, 16, held0)
            terms(part, 18, held1, 1)

    def slopes(i):
        rows = block(i, 128)
        for k in range(6):
            v = hid[k, rows, :].astype(F32)
            part, t = gelu_parts(v)
            inner = ROOT * (1.0 + 3.0 * CUBIC * (v * v))
            slope[rows, k * 128 : (k + 1) * 128] = part + 0.5 * v * ((1.0 - t * t) * inner)
            act_t[k * 128 : (k + 1) * 128, rows] = jnp.transpose(v * part).astype(BF16)

    found = [[] for _ in range(PARTS)]

    def totals(part):
        cols = slice(part * PART, part * PART + PART)
        pair = jnp.concatenate(
            [
                jnp.sum(sums[0, :, cols], axis=0, keepdims=True),
                jnp.sum(sums[1, :, cols], axis=0, keepdims=True) * (LOGIT_SCALE / STEP),
            ],
            axis=0,
        )
        return pair_sums(
            place, pair, got.at[part], pair_send.at[part], pair_recv.at[part], found[part]
        )

    def settle(part):
        total, target = found[part][0][0:1, :], found[part][0][1:2, :]
        target = target - LOGIT_SCALE * COS_MARGIN
        mean = jnp.sum(LOGIT_SCALE + jnp.log(total) - target, axis=1, keepdims=True) * (1.0 / IMAGES)
        loss[...] = mean if part == 0 else loss[...] + mean
        sums[0, 0:1, part * PART : part * PART + PART] = FACTOR / total
        gut[...] = jnp.zeros_like(gut)

    def coeffs(part, start, held, tiles=2):
        for k in range(tiles):
            i = start + k
            rows = block(i, TILE)
            column = columns(i)
            for low in range(0, PART, 128):
                cols = slice(part * PART + low, part * PART + low + 128)
                picked = jnp.where(column == places[:, cols], FACTOR, 0.0)
                coeff = expt[rows, cols].astype(F32) * sums[0, 0:1, cols] - picked
                coeff = coeff.astype(BF16)
                expt[rows, cols] = coeff
                held[k * TILE : (k + 1) * TILE, low : low + 128] = coeff

    def weigh(start, held, tiles=2):
        cols = pl.ds(pl.multiple_of(start * TILE, TILE), tiles * TILE)
        gut[...] += jnp.dot(nht[:, cols], held[: tiles * TILE, :], preferred_element_type=F32)

    def backward(part, low, high):
        if low == 0:
            settle(part)
            coeffs(part, 0, pair0)

        def step(i):
            weigh(4 * i, pair0)
            coeffs(part, 4 * i + 2, pair1)
            weigh(4 * i + 2, pair1)
            coeffs(part, 4 * i + 4, pair0)

        each(high - low, step, low)
        if high == 4:
            weigh(16, pair0)
            coeffs(part, 18, pair1, 1)
            weigh(18, pair1, 1)

    def split(part):
        acc, s0 = two[part][0], two[part][1]

        def step(i):
            rows = block(i, 128)
            for g in range(2):
                mine = block(place.core * 2 + g, 128)
                theirs = block((1 - place.core) * 2 + g, 128)
                acc[g, rows, :] = jnp.transpose(gut[mine, rows])
                s0[g, rows, :] = jnp.transpose(gut[theirs, rows])

        each(2, step)
        return sum_everywhere(place, part, 2, ORDERS[1], two[part], gu)

    done = [0]

    def pull(i, held):
        held[...] = jnp.dot(expt[block(i, TILE), :], uh[...], preferred_element_type=F32)

    def centre(i, held):
        rows = block(i, TILE)
        cen = centres[rows, :].astype(F32)
        inv = lax.rsqrt(jnp.sum(cen * cen, axis=1, keepdims=True) + NORM_EPSILON)
        normed = cen * inv
        grad_normed = held[...]
        along = jnp.sum(grad_normed * normed, axis=1, keepdims=True)
        nh[rows, :] = (inv * (grad_normed - normed * along)).astype(BF16)
        pltpu.make_async_copy(nh.at[rows], grad_centres.at[rows], out_sem.at[0]).start()

    def centre_grads(count):
        if done[0] == 0:
            pull(0, wide0)

        def step(i):
            pull(2 * i + 1, wide1)
            centre(2 * i, wide0)
            pull(2 * i + 2, wide0)
            centre(2 * i + 1, wide1)

        each(count, step, done[0])
        done[0] += count
        if done[0] == 9:
            centre(18, wide0)

    def finish(part):
        rows = slice(part * PART, part * PART + PART)
        g = jnp.concatenate([gu[k, rows, :] for k in range(4)], axis=1).astype(F32)
        u = uh[rows, :].astype(F32)
        along = jnp.sum(g * u, axis=1, keepdims=True)
        grad_embed = (inv_embed[rows, :] * (g - u * along)).astype(BF16)
        ge[rows, :] = grad_embed
        grad_act = lax.dot_general(
            grad_embed, second[...], (((1,), (1,)), ((), ())), preferred_element_type=F32
        )
        act[rows, :] = (grad_act * slope[rows, :]).astype(BF16)

    def early(_):
        known = slice(0, IMAGES - PART)

        def rows_of_first(i):
            rows = block(i, 288)
            first[rows, :] = jnp.dot(turned[rows, known], act[known, :], preferred_element_type=F32)

        each(3, rows_of_first)

    def late(_):
        new = slice(IMAGES - PART, IMAGES)

        def rows_of_first(i):
            rows = block(i, 288)
            more = jnp.dot(turned[rows, new], act[new, :], preferred_element_type=F32)
            turned[rows, 0:HIDDEN] = (first[rows, :] + more).astype(BF16)

        def rows_of_second(i):
            rows = block(i, 256)
            act_t[rows, 0:EMBED] = jnp.dot(act_t[rows, :], ge[...], preferred_element_type=F32).astype(BF16)

        each(3, rows_of_first)
        leaving = [pltpu.make_async_copy(turned.at[:, pl.ds(0, HIDDEN)], grad_first, local_sem.at[4])]
        leaving[0].start()
        each(3, rows_of_second)
        leaving.append(pltpu.make_async_copy(act_t.at[:, pl.ds(0, EMBED)], grad_second, local_sem.at[5]))
        leaving[1].start()
        return leaving

    def go(steps):
        next(steps, None)

    c, t, r = [None] * PARTS, [None] * PARTS, [None] * PARTS

    def begin(part):
        c[part] = product(part)
        go(c[part])

    def count(part):
        t[part] = totals(part)
        go(t[part])

    def reduce(part):
        r[part] = split(part)
        go(r[part])

    each(24, normalise)
    exchange(1)
    each(CENTRES // 128 - 24, normalise, 24)
    loads[2].wait()
    begin(0)
    each(2, turn)
    go(c[0])
    exchange(2)
    each(19, locate)
    begin(1)
    go(c[0])
    exchange(3)
    each(2, turn, 2)
    go(c[1])
    each(19, locate, 19)
    spots[...] = jnp.max(where_found[...], axis=0, keepdims=True).astype(jnp.int32)
    go(c[0])
    begin(2)
    go(c[1])
    each(2, turn, 4)
    go(c[2])
    go(c[0])
    go(c[1])
    go(c[0])
    go(c[2])
    begin(3)
    each(2, turn, 6)
    go(c[1])
    go(c[3])
    loads[3].wait()
    go(c[0])
    go(c[2])
    go(c[0])
    embed(0)
    go(c[1])
    go(c[3])
    forward(0, 0, 2)
    go(c[2])
    forward(0, 2, 4)
    count(0)
    go(c[1])
    go(c[3])
    go(c[1])
    embed(1)
    go(c[2])
    go(t[0])
    forward(1, 0, 2)
    go(c[3])
    forward(1, 2, 4)
    count(1)
    go(t[0])
    go(c[2])
    go(c[2])
    embed(2)
    go(t[1])
    go(c[3])
    forward(2, 0, 2)
    go(t[0])
    forward(2, 2, 4)
    count(2)
    go(c[3])
    go(t[1])
    go(c[3])
    embed(3)
    go(t[2])
    forward(3, 0, 2)
    go(t[0])
    go(t[1])
    forward(3, 2, 4)
    count(3)
    go(t[2])
    backward(0, 0, 2)
    go(t[3])
    go(t[1])
    backward(0, 2, 4)
    reduce(0)
    go(t[2])
    backward(1, 0, 2)
    go(r[0])
    go(t[3])
    backward(1, 2, 4)
    reduce(1)
    go(t[2])
    each(2, slopes)
    go(r[1])
    backward(2, 0, 2)
    go(r[0])
    go(t[3])
    backward(2, 2, 4)
    reduce(2)
    go(r[1])
    each(2, slopes, 2)
    go(r[0])
    go(r[2])
    each(2, slopes, 4)
    go(t[3])
    backward(3, 0, 2)
    go(r[1])
    go(r[0])
    go(r[2])
    backward(3, 2, 4)
    reduce(3)
    each(2, slopes, 6)
    go(r[0])
    go(r[3])
    go(r[1])
    go(r[2])
    centre_grads(2)
    go(r[0])
    go(r[1])
    go(r[0])
    go(r[2])
    finish(0)
    go(r[3])
    centre_grads(1)
    go(r[1])
    go(r[2])
    centre_grads(1)
    go(r[1])
    go(r[3])
    finish(1)
    centre_grads(1)
    go(r[2])
    go(r[3])
    go(r[2])
    finish(2)
    centre_grads(1)
    early(0)
    go(r[3])
    centre_grads(2)
    go(r[3])
    centre_grads(1)
    go(r[3])
    finish(3)
    leaving = late(0)

    for part in range(PARTS):
        landed(blocks.at[pl.ds(0, 7 * SHARE)], a2a_send.at[part])
    for copy in leaving:
        copy.wait()
    landed(nh, out_sem.at[0])


def last_kernel(
    first_hbm, second_hbm, centres_hbm, loss_in,
    loss, grad_first, grad_second, grad_centres,
    first, second, held, in_sem, out_sem,
):
    parts = [pl.ds(k * (CENTRES // 8), CENTRES // 8) for k in range(8)]
    ways = [(centres_hbm.at[p], held.at[p], grad_centres.at[p]) for p in parts]
    ways += [(first_hbm, first, grad_first), (second_hbm, second, grad_second)]
    arrive = [pltpu.make_async_copy(w[0], w[1], in_sem.at[k]) for k, w in enumerate(ways)]
    depart = [pltpu.make_async_copy(w[1], w[2], out_sem.at[k]) for k, w in enumerate(ways)]
    for copy in arrive:
        copy.start()
    loss[...] = loss_in[...]
    for there, back in zip(arrive, depart):
        there.wait()
        back.start()
    for copy in depart:
        copy.wait()


def shards(features, first_weight, second_weight, centres, active, labels):
    in_place = pl.BlockSpec(memory_space=pl.ANY)
    near = pl.BlockSpec(memory_space=pltpu.VMEM)
    dma = pltpu.SemaphoreType.DMA
    loss, first, second, grads = pl.pallas_call(
        step_kernel,
        out_shape=(
            jax.ShapeDtypeStruct((1, 1), F32),
            jax.ShapeDtypeStruct((BLOCK, HIDDEN), BF16),
            jax.ShapeDtypeStruct((HIDDEN, EMBED), BF16),
            jax.ShapeDtypeStruct((CENTRES, EMBED), BF16),
        ),
        in_specs=[in_place] * 4 + [near] * 2,
        out_specs=(near,) + (in_place,) * 3,
        scratch_shapes=[
            pltpu.VMEM((128, 8 * BLOCK), BF16),
            pltpu.VMEM((BLOCK, HIDDEN), BF16),
            pltpu.VMEM((HIDDEN, EMBED), BF16),
            pltpu.VMEM((CENTRES, EMBED), BF16),
            pltpu.VMEM((8, 128, BLOCK), BF16),
            pltpu.VMEM((IMAGES, BLOCK), BF16),
            pltpu.VMEM((BLOCK, IMAGES), BF16),
            pltpu.VMEM((CENTRES, EMBED), BF16),
            pltpu.VMEM((EMBED, CENTRES), BF16),
            pltpu.VMEM((CENTRES, IMAGES), BF16),
            pltpu.VMEM((6, IMAGES, 128), BF16),
            pltpu.VMEM((IMAGES, HIDDEN), BF16),
            pltpu.VMEM((HIDDEN, IMAGES), BF16),
            pltpu.VMEM((IMAGES, HIDDEN), F32),
            pltpu.VMEM((IMAGES, EMBED), BF16),
            pltpu.VMEM((IMAGES, 1), F32),
            pltpu.VMEM((4, IMAGES, 128), BF16),
            pltpu.VMEM((IMAGES, EMBED), BF16),
            pltpu.VMEM((BLOCK, HIDDEN), F32),
            pltpu.VMEM((2, 8, IMAGES), F32),
            pltpu.VMEM((PARTS, 4, 4, 2, PART), F32),
            pltpu.VMEM((1, IMAGES), jnp.int32),
            pltpu.VMEM((1, IMAGES), jnp.int32),
            pltpu.VMEM((8, IMAGES), F32),
            pltpu.VMEM((2 * TILE, PART), F32),
            pltpu.VMEM((2 * TILE, PART), F32),
            pltpu.VMEM((TILE, EMBED), F32),
            pltpu.VMEM((TILE, EMBED), F32),
            pltpu.VMEM((2 * TILE, PART), BF16),
            pltpu.VMEM((2 * TILE, PART), BF16),
            dma((6,)),
            dma((1,)),
            dma((PARTS,)),
            dma((PARTS,)),
            dma((PARTS, 4)),
            dma((PARTS, 4)),
        ]
        + sum_scratch(3) * PARTS
        + sum_scratch(2) * PARTS,
        compiler_params=pltpu.CompilerParams(
            collective_id=0, has_side_effects=True, vmem_limit_bytes=67043328
        ),
    )(
        features,
        first_weight,
        second_weight,
        centres,
        active.reshape(1, CENTRES),
        labels.reshape(1, IMAGES),
    )
    loss, grad_first, grad_second, grad_centres = pl.pallas_call(
        last_kernel,
        out_shape=(
            jax.ShapeDtypeStruct((1, 1), F32),
            jax.ShapeDtypeStruct((BLOCK, HIDDEN), BF16),
            jax.ShapeDtypeStruct((HIDDEN, EMBED), BF16),
            jax.ShapeDtypeStruct((CENTRES, EMBED), BF16),
        ),
        in_specs=[in_place] * 3 + [near],
        out_specs=(near,) + (in_place,) * 3,
        scratch_shapes=[
            pltpu.VMEM((BLOCK, HIDDEN), BF16),
            pltpu.VMEM((HIDDEN, EMBED), BF16),
            pltpu.VMEM((CENTRES, EMBED), BF16),
            dma((10,)),
            dma((10,)),
        ],
        compiler_params=pltpu.CompilerParams(vmem_limit_bytes=60000000),
    )(first, second, grads, loss)
    return loss.reshape(()), grad_first, grad_second, grad_centres


def solution(mesh):
    placed = (
        P("gx", "gy"),
        P(("gy", "gx"), None),
        P(),
        P(("gx", "gy"), None),
        P(("gx", "gy")),
        P(),
    )
    return jax.shard_map(
        shards,
        mesh=mesh,
        in_specs=placed,
        out_specs=(P(), P(("gy", "gx"), None), P(), P(("gx", "gy"), None)),
        check_vma=False,
    )
```

```python
import jax
import jax.numpy as jnp
import numpy as np
from jax import lax
from jax.experimental import pallas as pl
from jax.experimental.pallas import tpu as pltpu
from jax.sharding import PartitionSpec as P

CLS_DEV = 16128
LOGIT_SCALE = 64.0
COS_MARGIN = 0.4
NORM_EPSILON = 1e-06

MESH = pl.DeviceIdType.MESH
BF16 = jnp.bfloat16
F32 = jnp.float32
IMAGES = 1024
HIDDEN = 768
EMBED = 512
BLOCK = 864
CENTRES = 4864
FACTOR = LOGIT_SCALE / IMAGES
SCALE = float(np.float32(LOGIT_SCALE * 1.4426950408889634))
MARGIN = SCALE * COS_MARGIN
STEP = float(np.float32(SCALE + MARGIN) - np.float32(SCALE))
ROOT = 0.7978845608028654
CUBIC = 0.044715
ORDERS = (
    (("u", "v", "y"), ("v", "u", "y"), ("u", "v", "y")),
    (("x", "y", "z"), ("y", "z", "x"), ("z", "x", "y")),
)
TILE = 256
PARTS = 4
PART = IMAGES // PARTS
SHARE = 128 // PARTS


class Place:
    def __init__(self):
        gx, gy = lax.axis_index("gx"), lax.axis_index("gy")
        self.gx, self.gy = gx, gy
        self.core = lax.rem(gx, 2)
        x, z = lax.rem(gy, 4), lax.div(gy, 4)
        u, v = x + self.core * (z - x), z + self.core * (x - z)
        self.pos = {"y": lax.div(gx, 2), "z": z, "x": x, "u": u, "v": v}

    def peer(self, axis, d):
        q = lax.rem(self.pos[axis] + d, 4)
        if axis == "y":
            return (q * 2 + self.core, self.gy)
        if axis in ("u", "v"):
            x, z = self.pos["x"], self.pos["z"]
            turned = self.core if axis == "u" else 1 - self.core
            return (self.gx, (z + turned * (q - z)) * 4 + x + (1 - turned) * (q - x))
        if axis == "z":
            return (self.gx, q * 4 + self.pos["x"])
        return (self.gx, self.pos["z"] * 4 + q)

    def partner(self):
        return (self.gx + 1 - 2 * self.core, self.gy)

    def row(self, d):
        return (lax.rem(self.gx + d, 8), self.gy)

    def greet(self, meanwhile):
        barrier = pltpu.get_barrier_semaphore()
        devices = [self.peer(axis, d) for axis in ("x", "z") for d in (1, 2, 3)]
        devices += [self.row(d) for d in range(1, 8)]
        for device in devices:
            pl.semaphore_signal(barrier, inc=1, device_id=device, device_id_type=MESH)
        meanwhile()
        pl.semaphore_wait(barrier, len(devices))


def remote(src, dst, send, recv, device):
    return pltpu.make_async_remote_copy(
        src_ref=src, dst_ref=dst, send_sem=send, recv_sem=recv, device_id=device, device_id_type=MESH
    )


def block(index, size):
    return pl.ds(pl.multiple_of(index * size, size), size)


def each(count, body, start=0):
    def step(i, carry):
        body(i)
        return carry

    lax.fori_loop(start, start + count, step, 0)


def sum_scratch(groups):
    return [
        pltpu.VMEM((groups, PART, 128), F32),
        pltpu.VMEM((groups, PART, 128), F32),
        pltpu.VMEM((groups, PART, 128), F32),
        pltpu.VMEM((groups, PART, 128), BF16),
        pltpu.VMEM((groups, 3, PART // 4, 128), BF16),
        pltpu.VMEM((groups, PART // 4, 128), F32),
        pltpu.VMEM((groups, 3, PART // 16, 128), F32),
        pltpu.VMEM((groups, 4, PART // 16, 128), F32),
        pltpu.SemaphoreType.DMA((7,)),
        pltpu.SemaphoreType.DMA((groups, 7)),
    ]


def landed(like, sem):
    pltpu.make_async_copy(like, like, sem).wait()


def sum_everywhere(place, part, groups, orders, bufs, out):
    acc, s0, r0, s1, r1, acc2, r2, x3, send, recv = bufs
    core = place.core
    like = (
        r0,
        r1,
        r2,
        x3.at[:, pl.ds(0, 3)],
        s1.at[:, pl.ds(0, 3 * (PART // 16))],
        r1,
        s1,
    )

    def go(src, dst, g, stage, device):
        remote(src, dst, send.at[stage], recv.at[g, stage], device).start()

    def scatter(g, stage, axis, sent, got, size):
        for d in (2, 1, 3):
            rows = block(lax.rem(place.pos[axis] + d, 4), size)
            go(sent.at[g, rows], got.at[g, d - 1], g, stage, place.peer(axis, d))

    def spread(g, stage, axis, base, size):
        piece = out.at[core * groups + g, pl.ds(pl.multiple_of(base, size), size)]
        for d in (2, 1, 3):
            go(piece, piece, g, stage, place.peer(axis, d))

    for g in range(groups):
        go(s0.at[g], r0.at[g], g, 0, place.partner())
    yield
    for g in range(groups):
        landed(like[0].at[g], recv.at[g, 0])

        def add(i, g=g):
            rows = block(i, 128)
            total = acc[g, rows, :] + r0[g, rows, :]
            acc[g, rows, :] = total
            s1[g, rows, :] = total.astype(BF16)

        each(2, add)
        scatter(g, 1, orders[g][0], s1, r1, PART // 4)
    landed(like[0], send.at[0])
    yield
    for g in range(groups):
        landed(like[1].at[g], recv.at[g, 1])
        own = block(place.pos[orders[g][0]], PART // 4)
        acc2[g] = acc[g, own, :] + (r1[g, 0].astype(F32) + r1[g, 1].astype(F32) + r1[g, 2].astype(F32))
        scatter(g, 2, orders[g][1], acc2, r2, PART // 16)
    landed(like[1], send.at[1])
    yield
    for g in range(groups):
        landed(like[2].at[g], recv.at[g, 2])
        own = block(place.pos[orders[g][1]], PART // 16)
        p = place.pos[orders[g][2]]
        x3[g, p] = acc2[g, own, :] + (r2[g, 0] + r2[g, 1] + r2[g, 2])
        slot = x3.at[g, p]
        for d in (2, 1, 3):
            go(slot, slot, g, 3, place.peer(orders[g][2], d))
    landed(like[2], send.at[2])
    yield
    bases = []
    for g in range(groups):
        landed(like[3].at[g], recv.at[g, 3])
        first = part * PART + place.pos[orders[g][0]] * (PART // 4)
        bases.append((first + place.pos[orders[g][1]] * (PART // 16), first))
        total = (x3[g, 0] + x3[g, 1]) + (x3[g, 2] + x3[g, 3])
        out[core * groups + g, pl.ds(pl.multiple_of(bases[g][0], PART // 16), PART // 16), :] = total.astype(BF16)
        spread(g, 4, orders[g][1], bases[g][0], PART // 16)
    landed(like[3], send.at[3])
    yield
    for g in range(groups):
        landed(like[4].at[g], recv.at[g, 4])
        spread(g, 5, orders[g][0], bases[g][1], PART // 4)
    landed(like[4], send.at[4])
    yield
    for g in range(groups):
        landed(like[5].at[g], recv.at[g, 5])
        whole = out.at[core * groups + g, pl.ds(part * PART, PART)]
        go(whole, whole, g, 6, place.partner())
    landed(like[5], send.at[5])
    yield
    for g in range(groups):
        landed(like[6].at[g], recv.at[g, 6])
    landed(like[6], send.at[6])


def pair_sums(place, value, got, send, recv, keep):
    for stage, axis in enumerate(("core", "x", "y", "z")):
        p = place.core if axis == "core" else place.pos[axis]
        got[stage, p] = value
        slot = got.at[stage, p]
        steps = (1,) if axis == "core" else (2, 1, 3)
        for d in steps:
            device = place.partner() if axis == "core" else place.peer(axis, d)
            remote(slot, slot, send.at[stage], recv.at[stage], device).start()
        yield
        like = got.at[stage, pl.ds(0, len(steps))]
        landed(like, recv.at[stage])
        value = got[stage, 0] + got[stage, 1]
        if axis != "core":
            value = value + (got[stage, 2] + got[stage, 3])
        landed(like, send.at[stage])
    keep.append(value)


def gelu_parts(v):
    t = jnp.tanh(ROOT * (v + CUBIC * (v * v * v)))
    return 0.5 * (1.0 + t), t


def step_kernel(
    features_hbm, weight_hbm, second_hbm, centres_hbm, active, labels,
    loss, grad_first, grad_second, nh,
    features, weight, second, centres, sends, blocks, turned, nht, expt,
    hid, act, act_t, slope, uh, inv_embed, gu, ge,
    sums, got, places, spots, where_found, held0, held1, pair0, pair1, local_sem, a2a_send, a2a_recv, pair_send, pair_recv, *bufs,
):
    size = len(bufs) // (2 * PARTS)
    sets = [bufs[k * size : (k + 1) * size] for k in range(2 * PARTS)]
    one, two = sets[:PARTS], sets[PARTS:]
    place = Place()
    me = place.gx
    device = me * 16 + place.gy
    gut = held0
    loads = [
        pltpu.make_async_copy(src, dst, local_sem.at[2 + i])
        for i, (src, dst) in enumerate(
            ((centres_hbm, centres), (weight_hbm, weight), (second_hbm, second))
        )
    ]

    def prepare():
        for k in range(2):
            wide = pltpu.make_async_copy(
                features_hbm.at[:, pl.ds(k * 4 * BLOCK, 4 * BLOCK)], features, local_sem.at[k]
            )
            wide.start()
            if k == 0:
                for load in loads:
                    load.start()
            wide.wait()
            for j in range(4):
                sends[4 * k + j] = features[:, j * BLOCK : (j + 1) * BLOCK]

    place.greet(prepare)
    def exchange(part):
        for d in (4, 5, 3, 2, 6, 7, 1):
            remote(
                sends.at[lax.rem(me + d, 8), pl.ds(part * SHARE, SHARE)],
                blocks.at[pl.ds(pl.multiple_of(part * PART + me * SHARE, SHARE), SHARE)],
                a2a_send.at[part],
                a2a_recv.at[part],
                place.row(d),
            ).start()

    exchange(0)
    for part in range(PARTS):
        low = part * SHARE
        blocks[pl.ds(pl.multiple_of(part * PART + me * SHARE, SHARE), SHARE), :] = sends[me, low : low + SHARE, :]
        for j in range(8):
            spot = part * PART + j * SHARE
            places[:, spot : spot + SHARE] = labels[:, j * 128 + low : j * 128 + low + SHARE]
    sums[...] = jnp.zeros_like(sums)
    where_found[...] = jnp.full_like(where_found, -1.0)
    loads[0].wait()

    def normalise(i):
        rows = block(i, 128)
        cen = centres[rows, :].astype(F32)
        normed = cen * lax.rsqrt(jnp.sum(cen * cen, axis=1, keepdims=True) + NORM_EPSILON)
        nh[rows, :] = normed.astype(BF16)
        nht[:, rows] = jnp.transpose(normed).astype(BF16)

    def product(part):
        acc, s0 = one[part][0], one[part][1]
        mine = pl.ds(pl.multiple_of(place.core * 384, 128), 384)
        theirs = pl.ds(pl.multiple_of((1 - place.core) * 384, 128), 384)
        landed(blocks.at[pl.ds(0, 7 * SHARE)], a2a_recv.at[part])
        piece = blocks[part * PART : part * PART + PART, :]
        other = jnp.dot(piece, weight[:, theirs], preferred_element_type=F32)
        own = jnp.dot(piece, weight[:, mine], preferred_element_type=F32)
        for g in range(3):
            acc[g] = own[:, g * 128 : (g + 1) * 128]
            s0[g] = other[:, g * 128 : (g + 1) * 128]
        return sum_everywhere(place, part, 3, ORDERS[part // 3], one[part], hid)

    def turn(i):
        rows = block(i, 128)
        for k in range(0, BLOCK, 128):
            top = min(k + 128, BLOCK)
            turned[k:top, rows] = jnp.transpose(blocks[rows, k:top].astype(F32)).astype(BF16)

    def embed(i):
        rows = block(i, 256)
        for k in range(6):
            v = hid[k, rows, :].astype(F32)
            act[rows, k * 128 : (k + 1) * 128] = (v * gelu_parts(v)[0]).astype(BF16)
        emb = jnp.dot(act[rows, :], second[...], preferred_element_type=F32)
        inv = lax.rsqrt(jnp.sum(emb * emb, axis=1, keepdims=True) + NORM_EPSILON)
        inv_embed[rows, :] = inv
        u = emb * inv
        uh[rows, :] = u.astype(BF16)

    def locate(i):
        row = active[block(i, 128)].reshape(1, 128) + device * CLS_DEV
        column = jnp.transpose(jnp.broadcast_to(row, (128, 128)))
        here = (lax.broadcasted_iota(jnp.int32, (128, 128), 0) + i * 128).astype(F32)
        for part in range(0, IMAGES, 128):
            cols = slice(part, part + 128)
            hit = jnp.where(column == places[:, cols], here, -1.0)
            best = jnp.max(hit.reshape(16, 8, 128), axis=0)
            where_found[:, cols] = jnp.maximum(where_found[:, cols], best)

    def columns(i):
        parts = []
        for k in range(TILE // 128):
            row = active[block(i * (TILE // 128) + k, 128)].reshape(1, 128) + device * CLS_DEV
            parts.append(jnp.transpose(jnp.broadcast_to(row, (128, 128))))
        return jnp.concatenate(parts, axis=0)

    def matches(i, imgs):
        spot = spots[:, imgs : imgs + 128] - i * TILE
        return lax.broadcasted_iota(jnp.int32, (TILE, 128), 0) == spot

    def cosines(part, start, held, tiles=2):
        rows = pl.ds(pl.multiple_of(start * TILE, TILE), tiles * TILE)
        held[: tiles * TILE, :] = lax.dot_general(
            nh[rows, :],
            uh[part * PART : part * PART + PART, :],
            (((1,), (1,)), ((), ())),
            preferred_element_type=F32,
        )

    def terms(part, start, held, tiles=2):
        for k in range(tiles):
            i = start + k
            rows = block(i, TILE)
            for low in range(0, PART, 128):
                cols = slice(part * PART + low, part * PART + low + 128)
                cosine = held[k * TILE : (k + 1) * TILE, low : low + 128]
                shift = jnp.where(matches(i, part * PART + low), SCALE + MARGIN, SCALE)
                exp_terms = jnp.exp2(SCALE * cosine - shift)
                hit = (shift - SCALE) * cosine
                sums[0, :, cols] += jnp.sum(exp_terms.reshape(TILE // 8, 8, 128), axis=0)
                sums[1, :, cols] += jnp.sum(hit.reshape(TILE // 8, 8, 128), axis=0)
                expt[rows, cols] = exp_terms.astype(BF16)

    def forward(part, low, high):
        if low == 0:
            cosines(part, 0, held0)

        def step(i):
            cosines(part, 4 * i + 2, held1)
            terms(part, 4 * i, held0)
            cosines(part, 4 * i + 4, held0)
            terms(part, 4 * i + 2, held1)

        each(high - low, step, low)
        if high == 4:
            cosines(part, 18, held1, 1)
            terms(part, 16, held0)
            terms(part, 18, held1, 1)

    def slopes(i):
        rows = block(i, 128)
        for k in range(6):
            v = hid[k, rows, :].astype(F32)
            part, t = gelu_parts(v)
            inner = ROOT * (1.0 + 3.0 * CUBIC * (v * v))
            slope[rows, k * 128 : (k + 1) * 128] = part + 0.5 * v * ((1.0 - t * t) * inner)
            act_t[k * 128 : (k + 1) * 128, rows] = jnp.transpose(v * part).astype(BF16)

    found = [[] for _ in range(PARTS)]

    def totals(part):
        cols = slice(part * PART, part * PART + PART)
        pair = jnp.concatenate(
            [
                jnp.sum(sums[0, :, cols], axis=0, keepdims=True),
                jnp.sum(sums[1, :, cols], axis=0, keepdims=True) * (LOGIT_SCALE / STEP),
            ],
            axis=0,
        )
        return pair_sums(
            place, pair, got.at[part], pair_send.at[part], pair_recv.at[part], found[part]
        )

    def settle(part):
        total, target = found[part][0][0:1, :], found[part][0][1:2, :]
        target = target - LOGIT_SCALE * COS_MARGIN
        mean = jnp.sum(LOGIT_SCALE + jnp.log(total) - target, axis=1, keepdims=True) * (1.0 / IMAGES)
        loss[...] = mean if part == 0 else loss[...] + mean
        sums[0, 0:1, part * PART : part * PART + PART] = FACTOR / total
        gut[...] = jnp.zeros_like(gut)

    def coeffs(part, start, held, tiles=2):
        for k in range(tiles):
            i = start + k
            rows = block(i, TILE)
            column = columns(i)
            for low in range(0, PART, 128):
                cols = slice(part * PART + low, part * PART + low + 128)
                picked = jnp.where(column == places[:, cols], FACTOR, 0.0)
                coeff = expt[rows, cols].astype(F32) * sums[0, 0:1, cols] - picked
                coeff = coeff.astype(BF16)
                expt[rows, cols] = coeff
                held[k * TILE : (k + 1) * TILE, low : low + 128] = coeff

    def weigh(start, held, tiles=2):
        cols = pl.ds(pl.multiple_of(start * TILE, TILE), tiles * TILE)
        gut[...] += jnp.dot(nht[:, cols], held[: tiles * TILE, :], preferred_element_type=F32)

    def backward(part, low, high):
        if low == 0:
            settle(part)
            coeffs(part, 0, pair0)

        def step(i):
            weigh(4 * i, pair0)
            coeffs(part, 4 * i + 2, pair1)
            weigh(4 * i + 2, pair1)
            coeffs(part, 4 * i + 4, pair0)

        each(high - low, step, low)
        if high == 4:
            weigh(16, pair0)
            coeffs(part, 18, pair1, 1)
            weigh(18, pair1, 1)

    def split(part):
        acc, s0 = two[part][0], two[part][1]

        def step(i):
            rows = block(i, 128)
            for g in range(2):
                mine = block(place.core * 2 + g, 128)
                theirs = block((1 - place.core) * 2 + g, 128)
                acc[g, rows, :] = jnp.transpose(gut[mine, rows])
                s0[g, rows, :] = jnp.transpose(gut[theirs, rows])

        each(2, step)
        return sum_everywhere(place, part, 2, ORDERS[1], two[part], gu)

    done = [0]

    def pull(i, held):
        result = jnp.dot(expt[block(i, TILE), :], uh[...], preferred_element_type=F32)
        held[:TILE, :] = result[:, :PART]
        held[TILE:, :] = result[:, PART:]

    def centre(i, held):
        rows = block(i, TILE)
        cen = centres[rows, :].astype(F32)
        inv = lax.rsqrt(jnp.sum(cen * cen, axis=1, keepdims=True) + NORM_EPSILON)
        normed = cen * inv
        grad_normed = jnp.concatenate([held[:TILE, :], held[TILE:, :]], axis=1)
        along = jnp.sum(grad_normed * normed, axis=1, keepdims=True)
        nh[rows, :] = (inv * (grad_normed - normed * along)).astype(BF16)

    def centre_grads(count):
        if done[0] == 0:
            pull(0, held0)

        def step(i):
            pull(2 * i + 1, held1)
            centre(2 * i, held0)
            pull(2 * i + 2, held0)
            centre(2 * i + 1, held1)

        each(count, step, done[0])
        done[0] += count
        if done[0] == 9:
            centre(18, held0)

    def finish(part):
        rows = slice(part * PART, part * PART + PART)
        g = jnp.concatenate([gu[k, rows, :] for k in range(4)], axis=1).astype(F32)
        u = uh[rows, :].astype(F32)
        along = jnp.sum(g * u, axis=1, keepdims=True)
        grad_embed = (inv_embed[rows, :] * (g - u * along)).astype(BF16)
        ge[rows, :] = grad_embed
        grad_act = lax.dot_general(
            grad_embed, second[...], (((1,), (1,)), ((), ())), preferred_element_type=F32
        )
        act[rows, :] = (grad_act * slope[rows, :]).astype(BF16)

    def weights():
        def rows_of_first(i):
            rows = block(i, 288)
            grad_first[rows, :] = jnp.dot(turned[rows, :], act[...], preferred_element_type=F32).astype(BF16)

        def rows_of_second(i):
            rows = block(i, 256)
            grad_second[rows, :] = jnp.dot(act_t[rows, :], ge[...], preferred_element_type=F32).astype(BF16)

        each(3, rows_of_first)
        each(3, rows_of_second)

    def go(steps):
        next(steps, None)

    c, t, r = [None] * PARTS, [None] * PARTS, [None] * PARTS

    def begin(part):
        c[part] = product(part)
        go(c[part])

    def count(part):
        t[part] = totals(part)
        go(t[part])

    def reduce(part):
        r[part] = split(part)
        go(r[part])

    each(24, normalise)
    exchange(1)
    each(CENTRES // 128 - 24, normalise, 24)
    loads[1].wait()
    begin(0)
    each(2, turn)
    go(c[0])
    exchange(2)
    each(19, locate)
    begin(1)
    go(c[0])
    exchange(3)
    each(2, turn, 2)
    go(c[1])
    each(19, locate, 19)
    spots[...] = jnp.max(where_found[...], axis=0, keepdims=True).astype(jnp.int32)
    go(c[0])
    begin(2)
    go(c[1])
    each(2, turn, 4)
    go(c[2])
    go(c[0])
    go(c[1])
    go(c[0])
    go(c[2])
    begin(3)
    each(2, turn, 6)
    go(c[1])
    go(c[3])
    loads[2].wait()
    go(c[0])
    go(c[2])
    go(c[0])
    embed(0)
    go(c[1])
    go(c[3])
    forward(0, 0, 2)
    go(c[2])
    forward(0, 2, 4)
    count(0)
    go(c[1])
    go(c[3])
    go(c[1])
    embed(1)
    go(c[2])
    go(t[0])
    forward(1, 0, 2)
    go(c[3])
    forward(1, 2, 4)
    count(1)
    go(t[0])
    go(c[2])
    go(c[2])
    embed(2)
    go(t[1])
    go(c[3])
    forward(2, 0, 2)
    go(t[0])
    forward(2, 2, 4)
    count(2)
    go(c[3])
    go(t[1])
    go(c[3])
    embed(3)
    go(t[2])
    forward(3, 0, 2)
    go(t[0])
    go(t[1])
    forward(3, 2, 4)
    count(3)
    go(t[2])
    backward(0, 0, 2)
    go(t[3])
    go(t[1])
    backward(0, 2, 4)
    reduce(0)
    go(t[2])
    backward(1, 0, 2)
    go(r[0])
    go(t[3])
    backward(1, 2, 4)
    reduce(1)
    go(t[2])
    each(2, slopes)
    go(r[1])
    backward(2, 0, 2)
    go(r[0])
    go(t[3])
    backward(2, 2, 4)
    reduce(2)
    go(r[1])
    each(2, slopes, 2)
    go(r[0])
    go(r[2])
    each(2, slopes, 4)
    go(t[3])
    backward(3, 0, 2)
    go(r[1])
    go(r[0])
    go(r[2])
    backward(3, 2, 4)
    reduce(3)
    each(2, slopes, 6)
    go(r[0])
    go(r[3])
    go(r[1])
    go(r[2])
    centre_grads(2)
    go(r[0])
    go(r[3])
    go(r[1])
    go(r[2])
    go(r[0])
    centre_grads(1)
    finish(0)
    centre_grads(1)
    go(r[3])
    go(r[1])
    go(r[2])
    centre_grads(1)
    go(r[1])
    finish(1)
    centre_grads(1)
    go(r[3])
    go(r[2])
    centre_grads(1)
    go(r[2])
    finish(2)
    go(r[3])
    centre_grads(2)
    go(r[3])
    go(r[3])
    finish(3)
    weights()

    for part in range(PARTS):
        landed(blocks.at[pl.ds(0, 7 * SHARE)], a2a_send.at[part])


def last_kernel(first, second, held, loss_in, loss, grad_first, grad_second, grad_centres, sem):
    parts = [pl.ds(k * (CENTRES // 4), CENTRES // 4) for k in range(4)]
    ways = [(held.at[p], grad_centres.at[p]) for p in parts] + [(first, grad_first), (second, grad_second)]
    copies = [pltpu.make_async_copy(src, dst, sem.at[k]) for k, (src, dst) in enumerate(ways)]
    for copy in copies:
        copy.start()
    loss[...] = loss_in[...]
    for copy in copies:
        copy.wait()


def shards(features, first_weight, second_weight, centres, active, labels):
    in_place = pl.BlockSpec(memory_space=pl.ANY)
    near = pl.BlockSpec(memory_space=pltpu.VMEM)
    dma = pltpu.SemaphoreType.DMA
    loss, first, second, grads = pl.pallas_call(
        step_kernel,
        out_shape=(
            jax.ShapeDtypeStruct((1, 1), F32),
            pltpu.VMEM((BLOCK, HIDDEN), BF16),
            pltpu.VMEM((HIDDEN, EMBED), BF16),
            pltpu.VMEM((CENTRES, EMBED), BF16),
        ),
        in_specs=[in_place] * 4 + [near] * 2,
        out_specs=(near,) * 4,
        scratch_shapes=[
            pltpu.VMEM((128, 4 * BLOCK), BF16),
            pltpu.VMEM((BLOCK, HIDDEN), BF16),
            pltpu.VMEM((HIDDEN, EMBED), BF16),
            pltpu.VMEM((CENTRES, EMBED), BF16),
            pltpu.VMEM((8, 128, BLOCK), BF16),
            pltpu.VMEM((IMAGES, BLOCK), BF16),
            pltpu.VMEM((BLOCK, IMAGES), BF16),
            pltpu.VMEM((EMBED, CENTRES), BF16),
            pltpu.VMEM((CENTRES, IMAGES), BF16),
            pltpu.VMEM((6, IMAGES, 128), BF16),
            pltpu.VMEM((IMAGES, HIDDEN), BF16),
            pltpu.VMEM((HIDDEN, IMAGES), BF16),
            pltpu.VMEM((IMAGES, HIDDEN), F32),
            pltpu.VMEM((IMAGES, EMBED), BF16),
            pltpu.VMEM((IMAGES, 1), F32),
            pltpu.VMEM((4, IMAGES, 128), BF16),
            pltpu.VMEM((IMAGES, EMBED), BF16),
            pltpu.VMEM((2, 8, IMAGES), F32),
            pltpu.VMEM((PARTS, 4, 4, 2, PART), F32),
            pltpu.VMEM((1, IMAGES), jnp.int32),
            pltpu.VMEM((1, IMAGES), jnp.int32),
            pltpu.VMEM((8, IMAGES), F32),
            pltpu.VMEM((2 * TILE, PART), F32),
            pltpu.VMEM((2 * TILE, PART), F32),
            pltpu.VMEM((2 * TILE, PART), BF16),
            pltpu.VMEM((2 * TILE, PART), BF16),
            dma((5,)),
            dma((PARTS,)),
            dma((PARTS,)),
            dma((PARTS, 4)),
            dma((PARTS, 4)),
        ]
        + sum_scratch(3) * PARTS
        + sum_scratch(2) * PARTS,
        compiler_params=pltpu.CompilerParams(
            collective_id=0, has_side_effects=True, vmem_limit_bytes=59600000
        ),
    )(
        features,
        first_weight,
        second_weight,
        centres,
        active,
        labels.reshape(1, IMAGES),
    )
    loss, grad_first, grad_second, grad_centres = pl.pallas_call(
        last_kernel,
        out_shape=(
            jax.ShapeDtypeStruct((1, 1), F32),
            jax.ShapeDtypeStruct((BLOCK, HIDDEN), BF16),
            jax.ShapeDtypeStruct((HIDDEN, EMBED), BF16),
            jax.ShapeDtypeStruct((CENTRES, EMBED), BF16),
        ),
        in_specs=[near] * 4,
        out_specs=(near,) + (in_place,) * 3,
        scratch_shapes=[dma((6,))],
        compiler_params=pltpu.CompilerParams(vmem_limit_bytes=16000000),
    )(first, second, grads, loss)
    return loss.reshape(()), grad_first, grad_second, grad_centres


def solution(mesh):
    placed = (
        P("gx", "gy"),
        P(("gy", "gx"), None),
        P(),
        P(("gx", "gy"), None),
        P(("gx", "gy")),
        P(),
    )
    return jax.shard_map(
        shards,
        mesh=mesh,
        in_specs=placed,
        out_specs=(P(), P(("gy", "gx"), None), P(), P(("gx", "gy"), None)),
        check_vma=False,
    )
```

```python
import jax
import jax.numpy as jnp
import numpy as np
from jax import lax
from jax.experimental import pallas as pl
from jax.experimental.pallas import tpu as pltpu
from jax.sharding import PartitionSpec as P

CLS_DEV = 16128
LOGIT_SCALE = 64.0
COS_MARGIN = 0.4
NORM_EPSILON = 1e-06

MESH = pl.DeviceIdType.MESH
BF16 = jnp.bfloat16
F32 = jnp.float32
IMAGES = 1024
HIDDEN = 768
EMBED = 512
BLOCK = 864
CENTRES = 4864
FACTOR = LOGIT_SCALE / IMAGES
SCALE = float(np.float32(LOGIT_SCALE * 1.4426950408889634))
MARGIN = SCALE * COS_MARGIN
STEP = float(np.float32(SCALE + MARGIN) - np.float32(SCALE))
ROOT = 0.7978845608028654
CUBIC = 0.044715
ORDERS = (
    (("u", "v", "y"), ("v", "u", "y"), ("u", "v", "y")),
    (("x", "y", "z"), ("y", "z", "x"), ("z", "x", "y")),
)
TILE = 256
PARTS = 4
PART = IMAGES // PARTS
SHARE = 128 // PARTS


class Place:
    def __init__(self):
        gx, gy = lax.axis_index("gx"), lax.axis_index("gy")
        self.gx, self.gy = gx, gy
        self.core = lax.rem(gx, 2)
        x, z = lax.rem(gy, 4), lax.div(gy, 4)
        u, v = x + self.core * (z - x), z + self.core * (x - z)
        self.pos = {"y": lax.div(gx, 2), "z": z, "x": x, "u": u, "v": v}

    def peer(self, axis, d):
        q = lax.rem(self.pos[axis] + d, 4)
        if axis == "y":
            return (q * 2 + self.core, self.gy)
        if axis in ("u", "v"):
            x, z = self.pos["x"], self.pos["z"]
            turned = self.core if axis == "u" else 1 - self.core
            return (self.gx, (z + turned * (q - z)) * 4 + x + (1 - turned) * (q - x))
        if axis == "z":
            return (self.gx, q * 4 + self.pos["x"])
        return (self.gx, self.pos["z"] * 4 + q)

    def partner(self):
        return (self.gx + 1 - 2 * self.core, self.gy)

    def row(self, d):
        return (lax.rem(self.gx + d, 8), self.gy)

    def greet(self, meanwhile):
        barrier = pltpu.get_barrier_semaphore()
        devices = [self.peer(axis, d) for axis in ("x", "z") for d in (1, 2, 3)]
        devices += [self.row(d) for d in range(1, 8)]
        for device in devices:
            pl.semaphore_signal(barrier, inc=1, device_id=device, device_id_type=MESH)
        meanwhile()
        pl.semaphore_wait(barrier, len(devices))


def remote(src, dst, send, recv, device):
    return pltpu.make_async_remote_copy(
        src_ref=src, dst_ref=dst, send_sem=send, recv_sem=recv, device_id=device, device_id_type=MESH
    )


def block(index, size):
    return pl.ds(pl.multiple_of(index * size, size), size)


def each(count, body, start=0):
    def step(i, carry):
        body(i)
        return carry

    lax.fori_loop(start, start + count, step, 0)


def sum_scratch(groups):
    return [
        pltpu.VMEM((groups, PART, 128), F32),
        pltpu.VMEM((groups, PART, 128), F32),
        pltpu.VMEM((groups, PART, 128), F32),
        pltpu.VMEM((groups, PART, 128), BF16),
        pltpu.VMEM((groups, 3, PART // 4, 128), BF16),
        pltpu.VMEM((groups, PART // 4, 128), F32),
        pltpu.VMEM((groups, 3, PART // 16, 128), F32),
        pltpu.VMEM((groups, 4, PART // 16, 128), F32),
        pltpu.SemaphoreType.DMA((7,)),
        pltpu.SemaphoreType.DMA((groups, 7)),
    ]


def landed(like, sem):
    pltpu.make_async_copy(like, like, sem).wait()


def sum_everywhere(place, part, groups, orders, bufs, out):
    acc, s0, r0, s1, r1, acc2, r2, x3, send, recv = bufs
    core = place.core
    like = (
        r0,
        r1,
        r2,
        x3.at[:, pl.ds(0, 3)],
        s1.at[:, pl.ds(0, 3 * (PART // 16))],
        r1,
        s1,
    )

    def go(src, dst, g, stage, device):
        remote(src, dst, send.at[stage], recv.at[g, stage], device).start()

    def scatter(g, stage, axis, sent, got, size):
        for d in (2, 1, 3):
            rows = block(lax.rem(place.pos[axis] + d, 4), size)
            go(sent.at[g, rows], got.at[g, d - 1], g, stage, place.peer(axis, d))

    def spread(g, stage, axis, base, size):
        piece = out.at[core * groups + g, pl.ds(pl.multiple_of(base, size), size)]
        for d in (2, 1, 3):
            go(piece, piece, g, stage, place.peer(axis, d))

    for g in range(groups):
        go(s0.at[g], r0.at[g], g, 0, place.partner())
    yield
    for g in range(groups):
        landed(like[0].at[g], recv.at[g, 0])

        def add(i, g=g):
            rows = block(i, 128)
            total = acc[g, rows, :] + r0[g, rows, :]
            acc[g, rows, :] = total
            s1[g, rows, :] = total.astype(BF16)

        each(2, add)
        scatter(g, 1, orders[g][0], s1, r1, PART // 4)
    landed(like[0], send.at[0])
    yield
    for g in range(groups):
        landed(like[1].at[g], recv.at[g, 1])
        own = block(place.pos[orders[g][0]], PART // 4)
        acc2[g] = acc[g, own, :] + (r1[g, 0].astype(F32) + r1[g, 1].astype(F32) + r1[g, 2].astype(F32))
        scatter(g, 2, orders[g][1], acc2, r2, PART // 16)
    landed(like[1], send.at[1])
    yield
    for g in range(groups):
        landed(like[2].at[g], recv.at[g, 2])
        own = block(place.pos[orders[g][1]], PART // 16)
        p = place.pos[orders[g][2]]
        x3[g, p] = acc2[g, own, :] + (r2[g, 0] + r2[g, 1] + r2[g, 2])
        slot = x3.at[g, p]
        for d in (2, 1, 3):
            go(slot, slot, g, 3, place.peer(orders[g][2], d))
    landed(like[2], send.at[2])
    yield
    bases = []
    for g in range(groups):
        landed(like[3].at[g], recv.at[g, 3])
        first = part * PART + place.pos[orders[g][0]] * (PART // 4)
        bases.append((first + place.pos[orders[g][1]] * (PART // 16), first))
        total = (x3[g, 0] + x3[g, 1]) + (x3[g, 2] + x3[g, 3])
        out[core * groups + g, pl.ds(pl.multiple_of(bases[g][0], PART // 16), PART // 16), :] = total.astype(BF16)
        spread(g, 4, orders[g][1], bases[g][0], PART // 16)
    landed(like[3], send.at[3])
    yield
    for g in range(groups):
        landed(like[4].at[g], recv.at[g, 4])
        spread(g, 5, orders[g][0], bases[g][1], PART // 4)
    landed(like[4], send.at[4])
    yield
    for g in range(groups):
        landed(like[5].at[g], recv.at[g, 5])
        whole = out.at[core * groups + g, pl.ds(part * PART, PART)]
        go(whole, whole, g, 6, place.partner())
    landed(like[5], send.at[5])
    yield
    for g in range(groups):
        landed(like[6].at[g], recv.at[g, 6])
    landed(like[6], send.at[6])


def pair_sums(place, value, got, send, recv, keep):
    for stage, axis in enumerate(("core", "x", "y", "z")):
        p = place.core if axis == "core" else place.pos[axis]
        got[stage, p] = value
        slot = got.at[stage, p]
        steps = (1,) if axis == "core" else (2, 1, 3)
        for d in steps:
            device = place.partner() if axis == "core" else place.peer(axis, d)
            remote(slot, slot, send.at[stage], recv.at[stage], device).start()
        yield
        like = got.at[stage, pl.ds(0, len(steps))]
        landed(like, recv.at[stage])
        value = got[stage, 0] + got[stage, 1]
        if axis != "core":
            value = value + (got[stage, 2] + got[stage, 3])
        landed(like, send.at[stage])
    keep.append(value)


def gelu_parts(v):
    t = jnp.tanh(ROOT * (v + CUBIC * (v * v * v)))
    return 0.5 * (1.0 + t), t


def step_kernel(
    features_hbm, weight_hbm, second_hbm, centres_hbm, active, labels,
    loss, grad_first, grad_second, nh,
    features, weight, second, centres, sends, blocks, turned, nht, expt,
    hid, act, act_t, slope, uh, inv_embed, gu, ge,
    sums, got, places, spots, where_found, held0, held1, pair0, pair1, local_sem, a2a_send, a2a_recv, pair_send, pair_recv, *bufs,
):
    size = len(bufs) // (2 * PARTS)
    sets = [bufs[k * size : (k + 1) * size] for k in range(2 * PARTS)]
    one, two = sets[:PARTS], sets[PARTS:]
    place = Place()
    me = place.gx
    device = me * 16 + place.gy
    gut = held0
    loads = [
        pltpu.make_async_copy(src, dst, local_sem.at[2 + i])
        for i, (src, dst) in enumerate(
            ((centres_hbm, centres), (weight_hbm, weight), (second_hbm, second))
        )
    ]

    def prepare():
        for k in range(2):
            wide = pltpu.make_async_copy(
                features_hbm.at[:, pl.ds(k * 4 * BLOCK, 4 * BLOCK)], features, local_sem.at[k]
            )
            wide.start()
            if k == 0:
                for load in loads:
                    load.start()
            wide.wait()
            for j in range(4):
                sends[4 * k + j] = features[:, j * BLOCK : (j + 1) * BLOCK]

    place.greet(prepare)
    def exchange(part):
        for d in (4, 5, 3, 2, 6, 7, 1):
            remote(
                sends.at[lax.rem(me + d, 8), pl.ds(part * SHARE, SHARE)],
                blocks.at[pl.ds(pl.multiple_of(part * PART + me * SHARE, SHARE), SHARE)],
                a2a_send.at[part],
                a2a_recv.at[part],
                place.row(d),
            ).start()

    exchange(0)
    for part in range(PARTS):
        low = part * SHARE
        blocks[pl.ds(pl.multiple_of(part * PART + me * SHARE, SHARE), SHARE), :] = sends[me, low : low + SHARE, :]
        for j in range(8):
            spot = part * PART + j * SHARE
            places[:, spot : spot + SHARE] = labels[:, j * 128 + low : j * 128 + low + SHARE]
    sums[...] = jnp.zeros_like(sums)
    where_found[...] = jnp.full_like(where_found, -1.0)
    loads[0].wait()

    def normalise(i):
        rows = block(i, 128)
        cen = centres[rows, :].astype(F32)
        normed = cen * lax.rsqrt(jnp.sum(cen * cen, axis=1, keepdims=True) + NORM_EPSILON)
        nh[rows, :] = normed.astype(BF16)
        nht[:, rows] = jnp.transpose(normed).astype(BF16)

    def product(part):
        acc, s0 = one[part][0], one[part][1]
        mine = pl.ds(pl.multiple_of(place.core * 384, 128), 384)
        theirs = pl.ds(pl.multiple_of((1 - place.core) * 384, 128), 384)
        landed(blocks.at[pl.ds(0, 7 * SHARE)], a2a_recv.at[part])
        piece = blocks[part * PART : part * PART + PART, :]
        other = jnp.dot(piece, weight[:, theirs], preferred_element_type=F32)
        own = jnp.dot(piece, weight[:, mine], preferred_element_type=F32)
        for g in range(3):
            acc[g] = own[:, g * 128 : (g + 1) * 128]
            s0[g] = other[:, g * 128 : (g + 1) * 128]
        return sum_everywhere(place, part, 3, ORDERS[part // 3], one[part], hid)

    def turn(i):
        rows = block(i, 128)
        for k in range(0, BLOCK, 128):
            top = min(k + 128, BLOCK)
            turned[k:top, rows] = jnp.transpose(blocks[rows, k:top].astype(F32)).astype(BF16)

    def embed(i):
        rows = block(i, 256)
        for k in range(6):
            v = hid[k, rows, :].astype(F32)
            act[rows, k * 128 : (k + 1) * 128] = (v * gelu_parts(v)[0]).astype(BF16)
        emb = jnp.dot(act[rows, :], second[...], preferred_element_type=F32)
        inv = lax.rsqrt(jnp.sum(emb * emb, axis=1, keepdims=True) + NORM_EPSILON)
        inv_embed[rows, :] = inv
        u = emb * inv
        uh[rows, :] = u.astype(BF16)

    def locate(i):
        row = active[block(i, 128)].reshape(1, 128) + device * CLS_DEV
        column = jnp.transpose(jnp.broadcast_to(row, (128, 128)))
        here = (lax.broadcasted_iota(jnp.int32, (128, 128), 0) + i * 128).astype(F32)
        for part in range(0, IMAGES, 128):
            cols = slice(part, part + 128)
            hit = jnp.where(column == places[:, cols], here, -1.0)
            best = jnp.max(hit.reshape(16, 8, 128), axis=0)
            where_found[:, cols] = jnp.maximum(where_found[:, cols], best)

    def columns(i):
        parts = []
        for k in range(TILE // 128):
            row = active[block(i * (TILE // 128) + k, 128)].reshape(1, 128) + device * CLS_DEV
            parts.append(jnp.transpose(jnp.broadcast_to(row, (128, 128))))
        return jnp.concatenate(parts, axis=0)

    def matches(i, imgs):
        spot = spots[:, imgs : imgs + 128] - i * TILE
        return lax.broadcasted_iota(jnp.int32, (TILE, 128), 0) == spot

    def cosines(part, start, held, tiles=2):
        rows = pl.ds(pl.multiple_of(start * TILE, TILE), tiles * TILE)
        held[: tiles * TILE, :] = lax.dot_general(
            nh[rows, :],
            uh[part * PART : part * PART + PART, :],
            (((1,), (1,)), ((), ())),
            preferred_element_type=F32,
        )

    def terms(part, start, held, tiles=2):
        for k in range(tiles):
            i = start + k
            rows = block(i, TILE)
            for low in range(0, PART, 128):
                cols = slice(part * PART + low, part * PART + low + 128)
                cosine = held[k * TILE : (k + 1) * TILE, low : low + 128]
                shift = jnp.where(matches(i, part * PART + low), SCALE + MARGIN, SCALE)
                exp_terms = jnp.exp2(SCALE * cosine - shift)
                hit = (shift - SCALE) * cosine
                sums[0, :, cols] += jnp.sum(exp_terms.reshape(TILE // 8, 8, 128), axis=0)
                sums[1, :, cols] += jnp.sum(hit.reshape(TILE // 8, 8, 128), axis=0)
                expt[rows, cols] = exp_terms.astype(BF16)

    def forward(part, low, high):
        if low == 0:
            cosines(part, 0, held0)

        def step(i):
            cosines(part, 4 * i + 2, held1)
            terms(part, 4 * i, held0)
            cosines(part, 4 * i + 4, held0)
            terms(part, 4 * i + 2, held1)

        each(high - low, step, low)
        if high == 4:
            cosines(part, 18, held1, 1)
            terms(part, 16, held0)
            terms(part, 18, held1, 1)

    def slopes(i):
        rows = block(i, 128)
        for k in range(6):
            v = hid[k, rows, :].astype(F32)
            part, t = gelu_parts(v)
            inner = ROOT * (1.0 + 3.0 * CUBIC * (v * v))
            slope[rows, k * 128 : (k + 1) * 128] = part + 0.5 * v * ((1.0 - t * t) * inner)
            act_t[k * 128 : (k + 1) * 128, rows] = jnp.transpose(v * part).astype(BF16)

    found = [[] for _ in range(PARTS)]

    def totals(part):
        cols = slice(part * PART, part * PART + PART)
        pair = jnp.concatenate(
            [
                jnp.sum(sums[0, :, cols], axis=0, keepdims=True),
                jnp.sum(sums[1, :, cols], axis=0, keepdims=True) * (LOGIT_SCALE / STEP),
            ],
            axis=0,
        )
        return pair_sums(
            place, pair, got.at[part], pair_send.at[part], pair_recv.at[part], found[part]
        )

    def settle(part):
        total, target = found[part][0][0:1, :], found[part][0][1:2, :]
        target = target - LOGIT_SCALE * COS_MARGIN
        mean = jnp.sum(LOGIT_SCALE + jnp.log(total) - target, axis=1, keepdims=True) * (1.0 / IMAGES)
        loss[...] = mean if part == 0 else loss[...] + mean
        sums[0, 0:1, part * PART : part * PART + PART] = FACTOR / total
        gut[...] = jnp.zeros_like(gut)

    def coeffs(part, start, held, tiles=2):
        for k in range(tiles):
            i = start + k
            rows = block(i, TILE)
            column = columns(i)
            for low in range(0, PART, 128):
                cols = slice(part * PART + low, part * PART + low + 128)
                picked = jnp.where(column == places[:, cols], FACTOR, 0.0)
                coeff = expt[rows, cols].astype(F32) * sums[0, 0:1, cols] - picked
                coeff = coeff.astype(BF16)
                expt[rows, cols] = coeff
                held[k * TILE : (k + 1) * TILE, low : low + 128] = coeff

    def weigh(start, held, tiles=2):
        cols = pl.ds(pl.multiple_of(start * TILE, TILE), tiles * TILE)
        gut[...] += jnp.dot(nht[:, cols], held[: tiles * TILE, :], preferred_element_type=F32)

    def backward(part, low, high):
        if low == 0:
            settle(part)
            coeffs(part, 0, pair0)

        def step(i):
            weigh(4 * i, pair0)
            coeffs(part, 4 * i + 2, pair1)
            weigh(4 * i + 2, pair1)
            coeffs(part, 4 * i + 4, pair0)

        each(high - low, step, low)
        if high == 4:
            weigh(16, pair0)
            coeffs(part, 18, pair1, 1)
            weigh(18, pair1, 1)

    def split(part):
        acc, s0 = two[part][0], two[part][1]

        def step(i):
            rows = block(i, 128)
            for g in range(2):
                mine = block(place.core * 2 + g, 128)
                theirs = block((1 - place.core) * 2 + g, 128)
                acc[g, rows, :] = jnp.transpose(gut[mine, rows])
                s0[g, rows, :] = jnp.transpose(gut[theirs, rows])

        each(2, step)
        return sum_everywhere(place, part, 2, ORDERS[1], two[part], gu)

    done = [0]

    def pull(i, held):
        result = jnp.dot(expt[block(i, TILE), :], uh[...], preferred_element_type=F32)
        held[:TILE, :] = result[:, :PART]
        held[TILE:, :] = result[:, PART:]

    def centre(i, held):
        rows = block(i, TILE)
        cen = centres[rows, :].astype(F32)
        inv = lax.rsqrt(jnp.sum(cen * cen, axis=1, keepdims=True) + NORM_EPSILON)
        normed = cen * inv
        grad_normed = jnp.concatenate([held[:TILE, :], held[TILE:, :]], axis=1)
        along = jnp.sum(grad_normed * normed, axis=1, keepdims=True)
        nh[rows, :] = (inv * (grad_normed - normed * along)).astype(BF16)

    def centre_grads(count):
        if done[0] == 0:
            pull(0, held0)

        def step(i):
            pull(2 * i + 1, held1)
            centre(2 * i, held0)
            pull(2 * i + 2, held0)
            centre(2 * i + 1, held1)

        each(count, step, done[0])
        done[0] += count
        if done[0] == 9:
            centre(18, held0)

    def finish(part):
        rows = slice(part * PART, part * PART + PART)
        g = jnp.concatenate([gu[k, rows, :] for k in range(4)], axis=1).astype(F32)
        u = uh[rows, :].astype(F32)
        along = jnp.sum(g * u, axis=1, keepdims=True)
        grad_embed = (inv_embed[rows, :] * (g - u * along)).astype(BF16)
        ge[rows, :] = grad_embed
        grad_act = lax.dot_general(
            grad_embed, second[...], (((1,), (1,)), ((), ())), preferred_element_type=F32
        )
        act[rows, :] = (grad_act * slope[rows, :]).astype(BF16)

    def early():
        known = slice(0, IMAGES - PART)

        def rows_of_first(i):
            rows = block(i, 288)
            grad_first[rows, :] = jnp.dot(
                turned[rows, known], act[known, :], preferred_element_type=F32
            ).astype(BF16)

        each(3, rows_of_first)
        for i in range(3):
            rows = slice(i * 256, i * 256 + 256)
            result = jnp.dot(act_t[rows, known], ge[known, :], preferred_element_type=F32)
            for n in range(4):
                one[n][0][i] = result[:, n * 128 : (n + 1) * 128]

    def late():
        new = slice(IMAGES - PART, IMAGES)

        def rows_of_first(i):
            rows = block(i, 288)
            more = jnp.dot(turned[rows, new], act[new, :], preferred_element_type=F32)
            grad_first[rows, :] = (grad_first[rows, :].astype(F32) + more).astype(BF16)

        each(3, rows_of_first)
        for i in range(3):
            rows = slice(i * 256, i * 256 + 256)
            more = jnp.dot(act_t[rows, new], ge[new, :], preferred_element_type=F32)
            known = jnp.concatenate([one[n][0][i] for n in range(4)], axis=1)
            grad_second[rows, :] = (known + more).astype(BF16)

    def go(steps):
        next(steps, None)

    c, t, r = [None] * PARTS, [None] * PARTS, [None] * PARTS

    def begin(part):
        c[part] = product(part)
        go(c[part])

    def count(part):
        t[part] = totals(part)
        go(t[part])

    def reduce(part):
        r[part] = split(part)
        go(r[part])

    each(24, normalise)
    exchange(1)
    each(CENTRES // 128 - 24, normalise, 24)
    loads[1].wait()
    begin(0)
    each(2, turn)
    go(c[0])
    exchange(2)
    each(19, locate)
    begin(1)
    go(c[0])
    exchange(3)
    each(2, turn, 2)
    go(c[1])
    each(19, locate, 19)
    spots[...] = jnp.max(where_found[...], axis=0, keepdims=True).astype(jnp.int32)
    go(c[0])
    begin(2)
    go(c[1])
    each(2, turn, 4)
    go(c[2])
    go(c[0])
    go(c[1])
    go(c[0])
    go(c[2])
    begin(3)
    each(2, turn, 6)
    go(c[1])
    go(c[3])
    loads[2].wait()
    go(c[0])
    go(c[2])
    go(c[0])
    embed(0)
    go(c[1])
    go(c[3])
    forward(0, 0, 2)
    go(c[2])
    forward(0, 2, 4)
    count(0)
    go(c[1])
    go(c[3])
    go(c[1])
    embed(1)
    go(c[2])
    go(t[0])
    forward(1, 0, 2)
    go(c[3])
    forward(1, 2, 4)
    count(1)
    go(t[0])
    go(c[2])
    go(c[2])
    embed(2)
    go(t[1])
    go(c[3])
    forward(2, 0, 2)
    go(t[0])
    forward(2, 2, 4)
    count(2)
    go(c[3])
    go(t[1])
    go(c[3])
    embed(3)
    go(t[2])
    forward(3, 0, 2)
    go(t[0])
    go(t[1])
    forward(3, 2, 4)
    count(3)
    go(t[2])
    backward(0, 0, 2)
    go(t[3])
    go(t[1])
    backward(0, 2, 4)
    reduce(0)
    go(t[2])
    backward(1, 0, 2)
    go(r[0])
    go(t[3])
    backward(1, 2, 4)
    reduce(1)
    go(t[2])
    each(2, slopes)
    go(r[1])
    backward(2, 0, 2)
    go(r[0])
    go(t[3])
    backward(2, 2, 4)
    reduce(2)
    go(r[1])
    each(2, slopes, 2)
    go(r[0])
    go(r[2])
    each(2, slopes, 4)
    go(t[3])
    backward(3, 0, 2)
    go(r[1])
    go(r[0])
    go(r[2])
    backward(3, 2, 4)
    reduce(3)
    each(2, slopes, 6)
    go(r[0])
    go(r[3])
    go(r[1])
    go(r[2])
    centre_grads(2)
    go(r[0])
    go(r[3])
    go(r[1])
    go(r[2])
    go(r[0])
    centre_grads(1)
    finish(0)
    centre_grads(1)
    go(r[3])
    go(r[1])
    go(r[2])
    centre_grads(1)
    go(r[1])
    finish(1)
    centre_grads(1)
    go(r[3])
    go(r[2])
    centre_grads(1)
    go(r[2])
    finish(2)
    go(r[3])
    centre_grads(1)
    early()
    go(r[3])
    centre_grads(1)
    go(r[3])
    finish(3)
    late()

    for part in range(PARTS):
        landed(blocks.at[pl.ds(0, 7 * SHARE)], a2a_send.at[part])


def last_kernel(first, second, held, loss_in, loss, grad_first, grad_second, grad_centres, sem):
    parts = [pl.ds(k * (CENTRES // 4), CENTRES // 4) for k in range(4)]
    ways = [(held.at[p], grad_centres.at[p]) for p in parts] + [(first, grad_first), (second, grad_second)]
    copies = [pltpu.make_async_copy(src, dst, sem.at[k]) for k, (src, dst) in enumerate(ways)]
    for copy in copies:
        copy.start()
    loss[...] = loss_in[...]
    for copy in copies:
        copy.wait()


def shards(features, first_weight, second_weight, centres, active, labels):
    in_place = pl.BlockSpec(memory_space=pl.ANY)
    near = pl.BlockSpec(memory_space=pltpu.VMEM)
    dma = pltpu.SemaphoreType.DMA
    loss, first, second, grads = pl.pallas_call(
        step_kernel,
        out_shape=(
            jax.ShapeDtypeStruct((1, 1), F32),
            pltpu.VMEM((BLOCK, HIDDEN), BF16),
            pltpu.VMEM((HIDDEN, EMBED), BF16),
            pltpu.VMEM((CENTRES, EMBED), BF16),
        ),
        in_specs=[in_place] * 4 + [near] * 2,
        out_specs=(near,) * 4,
        scratch_shapes=[
            pltpu.VMEM((128, 4 * BLOCK), BF16),
            pltpu.VMEM((BLOCK, HIDDEN), BF16),
            pltpu.VMEM((HIDDEN, EMBED), BF16),
            pltpu.VMEM((CENTRES, EMBED), BF16),
            pltpu.VMEM((8, 128, BLOCK), BF16),
            pltpu.VMEM((IMAGES, BLOCK), BF16),
            pltpu.VMEM((BLOCK, IMAGES), BF16),
            pltpu.VMEM((EMBED, CENTRES), BF16),
            pltpu.VMEM((CENTRES, IMAGES), BF16),
            pltpu.VMEM((6, IMAGES, 128), BF16),
            pltpu.VMEM((IMAGES, HIDDEN), BF16),
            pltpu.VMEM((HIDDEN, IMAGES), BF16),
            pltpu.VMEM((IMAGES, HIDDEN), F32),
            pltpu.VMEM((IMAGES, EMBED), BF16),
            pltpu.VMEM((IMAGES, 1), F32),
            pltpu.VMEM((4, IMAGES, 128), BF16),
            pltpu.VMEM((IMAGES, EMBED), BF16),
            pltpu.VMEM((2, 8, IMAGES), F32),
            pltpu.VMEM((PARTS, 4, 4, 2, PART), F32),
            pltpu.VMEM((1, IMAGES), jnp.int32),
            pltpu.VMEM((1, IMAGES), jnp.int32),
            pltpu.VMEM((8, IMAGES), F32),
            pltpu.VMEM((2 * TILE, PART), F32),
            pltpu.VMEM((2 * TILE, PART), F32),
            pltpu.VMEM((2 * TILE, PART), BF16),
            pltpu.VMEM((2 * TILE, PART), BF16),
            dma((5,)),
            dma((PARTS,)),
            dma((PARTS,)),
            dma((PARTS, 4)),
            dma((PARTS, 4)),
        ]
        + sum_scratch(3) * PARTS
        + sum_scratch(2) * PARTS,
        compiler_params=pltpu.CompilerParams(
            collective_id=0, has_side_effects=True, vmem_limit_bytes=59600000
        ),
    )(
        features,
        first_weight,
        second_weight,
        centres,
        active,
        labels.reshape(1, IMAGES),
    )
    loss, grad_first, grad_second, grad_centres = pl.pallas_call(
        last_kernel,
        out_shape=(
            jax.ShapeDtypeStruct((1, 1), F32),
            jax.ShapeDtypeStruct((BLOCK, HIDDEN), BF16),
            jax.ShapeDtypeStruct((HIDDEN, EMBED), BF16),
            jax.ShapeDtypeStruct((CENTRES, EMBED), BF16),
        ),
        in_specs=[near] * 4,
        out_specs=(near,) + (in_place,) * 3,
        scratch_shapes=[dma((6,))],
        compiler_params=pltpu.CompilerParams(vmem_limit_bytes=16000000),
    )(first, second, grads, loss)
    return loss.reshape(()), grad_first, grad_second, grad_centres


def solution(mesh):
    placed = (
        P("gx", "gy"),
        P(("gy", "gx"), None),
        P(),
        P(("gx", "gy"), None),
        P(("gx", "gy")),
        P(),
    )
    return jax.shard_map(
        shards,
        mesh=mesh,
        in_specs=placed,
        out_specs=(P(), P(("gy", "gx"), None), P(), P(("gx", "gy"), None)),
        check_vma=False,
    )
```
